32 devices in a mesh: dp: 16 (over z, y, x), tensor: 2 (over core).
Axes of the slice: x: 2, y: 2, z: 4, core: 2. Of those that a mesh axis runs over, the one named last changes fastest.
Arguments:
- tokens: bfloat16 [32, 256, 1536], P('dp'), may hold values from -6 to 6
- context: bfloat16 [32, 130, 768], P('dp'), may hold values from -6 to 6
- live_count: int32 [16], P('dp'), may hold values from 1 to 2, as said below
- cotangent: bfloat16 [32, 256, 1536], P('dp'), may hold values from -6 to 6
- triple_weight: bfloat16 [1536, 3, 1536], P('dp', None, 'tensor'), may hold values from -0.15625 to 0.15625
- attn_out_weight: bfloat16 [1536, 1536], P('tensor', 'dp'), may hold values from -0.4375 to 0.4375
- cross_query_weight: bfloat16 [1536, 1536], P('dp', 'tensor'), may hold values from -0.15625 to 0.15625
- cross_pair_weight: bfloat16 [768, 2, 1536], P('dp', None, 'tensor'), may hold values from -0.21875 to 0.21875
- cross_out_weight: bfloat16 [1536, 1536], P('tensor', 'dp'), may hold values from -0.4375 to 0.4375
- gate_up_weight: bfloat16 [1536, 2, 6144], P('dp', None, 'tensor'), may hold values from -0.15625 to 0.15625
- down_weight: bfloat16 [6144, 1536], P('tensor', 'dp'), may hold values from -0.078125 to 0.078125
- norm_gains: bfloat16 [3, 1536], P(None, 'dp'), may hold values from 0.099609375 to 1.8984375
- norm_shifts: bfloat16 [3, 1536], P(None, 'dp'), may hold values from -3 to 3
Outputs:
- mixed: bfloat16 [32, 256, 1536], P('dp')
- grad_tokens: float32 [32, 256, 1536], P('dp')
- grad_context: float32 [32, 130, 768], P('dp')
- grad_triple: float32 [1536, 3, 1536], P('dp', None, 'tensor')
- grad_attn_out: float32 [1536, 1536], P('tensor', 'dp')
- grad_cross_query: float32 [1536, 1536], P('dp', 'tensor')
- grad_cross_pair: float32 [768, 2, 1536], P('dp', None, 'tensor')
- grad_cross_out: float32 [1536, 1536], P('tensor', 'dp')
- grad_gate_up: float32 [1536, 2, 6144], P('dp', None, 'tensor')
- grad_down: float32 [6144, 1536], P('tensor', 'dp')
- grad_gains: float32 [3, 1536], P(None, 'dp')
- grad_shifts: float32 [3, 1536], P(None, 'dp')
The draws below stay inside these ranges and needn't reach their ends.
Inputs may be any that keep to these rules, and one draw needn't show every extreme that they name: Slot m of a dp index is live exactly when m < its live_count; some index has 2 live slots and some has 1.
All inputs are finite; a program needn't handle non-finite values.
Results may differ from the reference program's by a relative error of at most 0.023.
Values may be sent and summed in bfloat16 or wider, within the bound.
No kernel may reach another device: no remote copies, remote signals or barrier semaphores. Data moves between devices by JAX's collectives and lax.ppermute only.
A program may use at most 256 MiB of HBM per device.

```python
import jax
import jax.numpy as jnp
from jax import lax

D = 1536
HD = 64
ROT = 32
FF = 6144
DC = 768
COND = 130
SEQ = 256
MB = 2
LAT = 32
N_DP = 16


def draw_live_count(key, part):
    counts = jax.random.randint(jax.random.fold_in(key, 11), (N_DP,), 1, MB + 1)
    shuffled = jax.random.permutation(jax.random.fold_in(key, 12), N_DP)
    counts = counts.at[shuffled[0]].set(MB)
    counts = counts.at[shuffled[1]].set(1)
    return counts.astype(jnp.int32)


def with_spikes(values, rng, source, target, shards_of, factor):
    def block_of(position):
        return (jnp.arange(values.shape[position]) // (values.shape[position] // shards_of)).reshape((-1,) + (1,) * (values.ndim - 1 - position))

    one_side = jax.random.permutation(rng, shards_of)[block_of(target)]
    second = (block_of(target) + shards_of // 2) % shards_of
    return jnp.where((block_of(source) == one_side) | (block_of(source) == second), factor * values, values)


def block_levels(key, dims, split, low, top_value):
    factor_of = 1.0
    for axis_at, parts in split:
        heights = jax.random.uniform(jax.random.fold_in(jax.random.fold_in(key, 6), axis_at), (parts,), jnp.float32, low / len(split), top_value / len(split))
        factor_of = factor_of * jnp.repeat(jnp.exp(heights), dims[axis_at] // parts).reshape((-1,) + (1,) * (len(dims) - 1 - axis_at))
    return factor_of


def gaussian(rng, dims, width, reach, shards=(), held_as=jnp.bfloat16):
    drawn = jax.random.normal(rng, dims, jnp.float32) * width
    if len(shards) > 0:
        drawn = block_levels(rng, dims, shards, -0.22, 0.18) * drawn
    return jnp.clip(drawn, min=-reach, max=reach).astype(held_as)


def gaussian_with(stream_key, shape, scale, most, pieces, heavy, kind=jnp.bfloat16):
    drawn = scale * jax.random.normal(stream_key, shape, jnp.float32)
    if pieces:
        drawn = drawn * block_levels(stream_key, shape, pieces, -0.22, 0.18)
    return jnp.clip(with_spikes(drawn, jax.random.fold_in(stream_key, 3), *heavy), -most, most).astype(kind)


def setup_inputs(seed: int = 0) -> dict:
    streams_of = jax.random.split(jax.random.key(seed), 14)
    tokens = gaussian_with(streams_of[0], (LAT, SEQ, D), 1.0, 6.0, ((0, 16),), (0, 2, 16, 2.0))
    context = gaussian(streams_of[1], (LAT, COND, DC), 1.0, 6.0, ((0, 16),))
    live_count = draw_live_count(jax.random.fold_in(streams_of[13], 71), 0)
    cotangent = gaussian_with(streams_of[3], (LAT, SEQ, D), 1.0, 6.0, ((0, 16),), (0, 2, 16, 2.0))
    triple_weight = gaussian(streams_of[4], (D, 3, D), D ** -0.5, 0.15625, ((0, 16), (2, 2)))
    attn_out_weight = gaussian(streams_of[5], (D, D), (D // 8) ** -0.5, 0.4375, ((0, 2), (1, 16)))
    cross_query_weight = gaussian(streams_of[6], (D, D), D ** -0.5, 0.15625, ((0, 16), (1, 2)))
    cross_pair_weight = gaussian(streams_of[7], (DC, 2, D), DC ** -0.5, 0.21875, ((0, 16), (2, 2)))
    cross_out_weight = gaussian(streams_of[8], (D, D), (D // 8) ** -0.5, 0.4375, ((0, 2), (1, 16)))
    gate_up_weight = gaussian(streams_of[9], (D, 2, FF), D ** -0.5, 0.15625, ((0, 16), (2, 2)))
    down_weight = gaussian(streams_of[10], (FF, D), FF ** -0.5, 0.078125, ((0, 2), (1, 16)))
    norm_gains = jnp.clip(1.0 + 0.18 * jax.random.normal(streams_of[11], (3, D), jnp.float32), 0.099609375, 1.8984375).astype(jnp.bfloat16)
    norm_shifts = gaussian(streams_of[12], (3, D), 0.5, 3.0, ((1, 16),))
    return dict(tokens=tokens, context=context, live_count=live_count, cotangent=cotangent, triple_weight=triple_weight, attn_out_weight=attn_out_weight, cross_query_weight=cross_query_weight, cross_pair_weight=cross_pair_weight, cross_out_weight=cross_out_weight, gate_up_weight=gate_up_weight, down_weight=down_weight, norm_gains=norm_gains, norm_shifts=norm_shifts)


EPSILON = 1e-05
HIGHEST = lax.Precision.HIGHEST

@jax.custom_vjp
def low(v):
    return lax.optimization_barrier(v.astype(jnp.bfloat16)).astype(jnp.float32)

@jax.custom_vjp
def low_back(v):
    return v

def low_keep(v):
    return (low(v), None)

def low_pass(kept, grad):
    return (grad,)

def back_keep(v):
    return (v, None)

def back_low(kept, grad):
    return (low(grad),)
low.defvjp(low_keep, low_pass)
low_back.defvjp(back_keep, back_low)

def norm_rows(values, gain_row, shift_row):
    average = lax.optimization_barrier(jnp.mean(values, axis=-1, keepdims=True))
    centred = values - average
    spread = lax.optimization_barrier(jnp.mean(centred * centred, axis=-1, keepdims=True))
    return centred * lax.rsqrt(spread + EPSILON) * gain_row + shift_row

def rotary_tables(length):
    half_dim = ROT // 2
    freqs = 10000.0 ** (-(2.0 * jnp.arange(half_dim, dtype=jnp.float32) / ROT))
    angles = jnp.arange(length, dtype=jnp.float32)[:, None] * freqs[None, :]
    return (jnp.cos(angles)[:, None, :], jnp.sin(angles)[:, None, :])

def rotate(values, cos_table, sin_table):
    half_dim = ROT // 2
    former = values[..., :half_dim]
    latter = values[..., half_dim:ROT]
    rest = values[..., ROT:]
    return jnp.concatenate([former * cos_table - latter * sin_table, latter * cos_table + former * sin_table, rest], axis=-1)

def attend(queries, key_rows, value_rows):
    scores = low_back(jnp.einsum('qhd,khd->hqk', queries, key_rows, precision=HIGHEST) * HD ** (-0.5))
    row_max = lax.optimization_barrier(jnp.max(scores, axis=-1, keepdims=True))
    exponent = jnp.exp(scores - row_max)
    prob_rows = low(exponent / lax.optimization_barrier(jnp.sum(exponent, axis=-1, keepdims=True)))
    mixed_rows = jnp.einsum('hqk,khd->qhd', prob_rows, value_rows, precision=HIGHEST)
    return low(low_back(mixed_rows))

def one_sequence(start, context, params, cos_table, sin_table):
    triple_w, attn_out_w, cross_query_w, cross_pair_w, cross_out_w, gate_up_w, down_w, gains, shifts = params
    length = start.shape[0]
    context_len = context.shape[0]
    head_count = D // HD
    input_one = low(norm_rows(start, gains[0], shifts[0]))
    triple = low_back(jnp.einsum('sd,dtf->stf', input_one, triple_w, precision=HIGHEST))
    queries = low(rotate(triple[:, 0].reshape(length, head_count, HD), cos_table, sin_table))
    key_rows = low(rotate(triple[:, 1].reshape(length, head_count, HD), cos_table, sin_table))
    value_rows = low(triple[:, 2].reshape(length, head_count, HD))
    mixed_one = attend(queries, key_rows, value_rows).reshape(length, D)
    first_sum = start + low_back(jnp.dot(mixed_one, attn_out_w, precision=HIGHEST))
    input_two = low(norm_rows(first_sum, gains[1], shifts[1]))
    cross_queries = low(low_back(jnp.dot(input_two, cross_query_w, precision=HIGHEST)).reshape(length, head_count, HD))
    pair_rows = low_back(jnp.einsum('cd,dtf->ctf', context, cross_pair_w, precision=HIGHEST))
    cross_keys = low(pair_rows[:, 0].reshape(context_len, head_count, HD))
    cross_values = low(pair_rows[:, 1].reshape(context_len, head_count, HD))
    mixed_two = attend(cross_queries, cross_keys, cross_values).reshape(length, D)
    second_sum = first_sum + low_back(jnp.dot(mixed_two, cross_out_w, precision=HIGHEST))
    input_three = low(norm_rows(second_sum, gains[2], shifts[2]))
    gate_up = low_back(jnp.einsum('sd,dtf->stf', input_three, gate_up_w, precision=HIGHEST))
    hidden = low(jax.nn.silu(gate_up[:, 0]) * gate_up[:, 1])
    return second_sum + low_back(jnp.dot(hidden, down_w, precision=HIGHEST))

def reference(tokens, context, live_count, cotangent, triple_weight, attn_out_weight, cross_query_weight, cross_pair_weight, cross_out_weight, gate_up_weight, down_weight, norm_gains, norm_shifts):
    cos_table, sin_table = rotary_tables(SEQ)
    latent_ids = jnp.arange(LAT, dtype=jnp.int32)
    owners = latent_ids // MB
    live_mask = (latent_ids % MB < live_count[owners]).astype(jnp.float32)

    def forward(start_all, context_all, triple_w, attn_out_w, cross_query_w, cross_pair_w, cross_out_w, gate_up_w, down_w, gains, shifts):
        params = (triple_w, attn_out_w, cross_query_w, cross_pair_w, cross_out_w, gate_up_w, down_w, gains, shifts)

        def single(pair_in):
            return one_sequence(pair_in[0], pair_in[1], params, cos_table, sin_table)
        outputs = lax.map(jax.checkpoint(single), (start_all, context_all))
        return outputs * live_mask[:, None, None]
    result, pull_back = jax.vjp(forward, tokens.astype(jnp.float32), context.astype(jnp.float32), triple_weight.astype(jnp.float32), attn_out_weight.astype(jnp.float32), cross_query_weight.astype(jnp.float32), cross_pair_weight.astype(jnp.float32), cross_out_weight.astype(jnp.float32), gate_up_weight.astype(jnp.float32), down_weight.astype(jnp.float32), norm_gains.astype(jnp.float32), norm_shifts.astype(jnp.float32))
    grad_tokens, grad_context, grad_triple, grad_attn_out, grad_cross_query, grad_cross_pair, grad_cross_out, grad_gate_up, grad_down, grad_gains, grad_shifts = pull_back(cotangent.astype(jnp.float32))
    return (result.astype(jnp.bfloat16), grad_tokens, grad_context, grad_triple, grad_attn_out, grad_cross_query, grad_cross_pair, grad_cross_out, grad_gate_up, grad_down, grad_gains, grad_shifts)
```

```python
import jax
import jax.numpy as jnp
import numpy as np
from jax import lax
from jax.sharding import Mesh
from jax.sharding import PartitionSpec as P

HD = 64
ROT = 32
EPSILON = 1e-05
F32 = jnp.float32
BF16 = jnp.bfloat16
DP = ("A", "B", "C")
T = "T"
FLIP = [(0, 1), (1, 0)]


def swap(value, axis):
    return lax.ppermute(value, axis, FLIP)


def dot(left, right, dims):
    return lax.dot_general(left, right, (dims, ((), ())), preferred_element_type=F32)


def nn(left, right):
    return dot(left, right, ((1,), (0,)))


def nt(left, right):
    return dot(left, right, ((1,), (1,)))


def tn(left, right):
    return dot(left, right, ((0,), (0,)))


def pick(flag, when_zero, when_one):
    return jnp.where(flag == 0, when_zero, when_one)


def to_rel(values, outer, b, c):
    lead = values.shape[:-1]
    n = len(lead)
    v = values.reshape(lead + (outer, 2, 2, -1))
    v = pick(b, v, jnp.flip(v, n + 1))
    v = pick(c, v, jnp.flip(v, n + 2))
    v = jnp.transpose(v, tuple(range(n)) + (n + 2, n + 1, n, n + 3))
    return v.reshape(values.shape)


def from_rel(values, outer, b, c):
    lead = values.shape[:-1]
    n = len(lead)
    v = values.reshape(lead + (2, 2, outer, -1))
    v = jnp.transpose(v, tuple(range(n)) + (n + 2, n + 1, n, n + 3))
    v = pick(b, v, jnp.flip(v, n + 1))
    v = pick(c, v, jnp.flip(v, n + 2))
    return v.reshape(values.shape)


def flip_half(values):
    half = values.shape[-1] // 2
    return jnp.concatenate([values[..., half:], values[..., :half]], axis=-1)


def gather_z(shard):
    return lax.all_gather(shard, "A", axis=0, tiled=True)


def scatter_z(rows):
    return lax.psum_scatter(rows, "A", scatter_dimension=0, tiled=True)


def gather_full(first):
    over_c = swap(first, "C")
    over_b = swap(first, "B")
    both = swap(over_b, "C")
    return jnp.concatenate([first, over_b, over_c, both], axis=0)


def gather_half(first):
    over_b = swap(first, "B")
    n = first.shape[1] // 2
    return jnp.concatenate([first[:, :n], over_b[:, :n], first[:, n:], over_b[:, n:]], axis=0)


def scatter_full(left, right):
    rows = left.shape[1]
    sent = swap(tn(left[:, rows // 2 :], right).astype(BF16), "C")
    q = rows // 4
    far = tn(left[:, q : 2 * q], right) + sent[q:].astype(F32)
    far = swap(far.astype(BF16), "B")
    near = tn(left[:, :q], right) + sent[:q].astype(F32) + far.astype(F32)
    return scatter_z(near.astype(BF16))


def scatter_half(left, right):
    rows = left.shape[1]
    q = rows // 4
    far = jnp.concatenate(
        [tn(left[:, q : 2 * q], right).astype(BF16), tn(left[:, 3 * q :], right).astype(BF16)],
        axis=1,
    )
    far = swap(far, "B")
    n = right.shape[1]
    near = jnp.concatenate(
        [
            (tn(left[:, :q], right) + far[:, :n].astype(F32)).astype(BF16),
            (tn(left[:, 2 * q : 3 * q], right) + far[:, n:].astype(F32)).astype(BF16),
        ],
        axis=1,
    )
    return scatter_z(near)


def norm_forward(values, gain_row, shift_row):
    average = jnp.mean(values, axis=-1, keepdims=True)
    centred = values - average
    spread = jnp.mean(centred * centred, axis=-1, keepdims=True)
    factor = lax.rsqrt(spread + EPSILON)
    normed = centred * factor
    return ((normed * gain_row + shift_row).astype(BF16), normed, factor)


def norm_backward(grad_rows, normed, factor, gain_row):
    scaled = grad_rows * gain_row
    first_mean = jnp.mean(scaled, axis=-1, keepdims=True)
    second_mean = jnp.mean(scaled * normed, axis=-1, keepdims=True)
    grad_values = factor * (scaled - first_mean - normed * second_mean)
    return (grad_values, jnp.sum(grad_rows * normed, axis=0), jnp.sum(grad_rows, axis=0))


def rotary_tables(length):
    half_dim = ROT // 2
    freqs = 10000.0 ** (-(2.0 * np.arange(half_dim, dtype=np.float32) / ROT))
    angles = np.arange(length, dtype=np.float32)[:, None] * freqs[None, :].astype(np.float32)
    return (
        jnp.asarray(np.cos(angles))[None, :, None, :],
        jnp.asarray(np.sin(angles))[None, :, None, :],
    )


def rotate(values, cos_table, sin_table):
    half_dim = ROT // 2
    former = values[..., :half_dim]
    latter = values[..., half_dim:ROT]
    rest = values[..., ROT:]
    return jnp.concatenate(
        [former * cos_table - latter * sin_table, latter * cos_table + former * sin_table, rest],
        axis=-1,
    )


def attend(q, k, v):
    scores = jnp.einsum("lqhd,lkhd->lhqk", q, k, preferred_element_type=F32) * HD ** (-0.5)
    row_max = jnp.max(scores, axis=-1, keepdims=True)
    exponent = jnp.exp(scores - row_max)
    row_sum = jnp.sum(exponent, axis=-1, keepdims=True)
    prob = (exponent / row_sum).astype(BF16)
    mixed = jnp.einsum("lhqk,lkhd->lqhd", prob, v, preferred_element_type=F32)
    return (mixed.astype(BF16), row_max + jnp.log(row_sum))


def attend_back(q, k, v, grad, logsum):
    scale = HD ** (-0.5)
    scores = jnp.einsum("lqhd,lkhd->lhqk", q, k, preferred_element_type=F32) * scale
    prob = jnp.exp(scores - logsum)
    grad_prob = jnp.einsum("lqhd,lkhd->lhqk", grad, v, preferred_element_type=F32)
    centre = jnp.sum(prob * grad_prob, axis=-1, keepdims=True)
    grad_scores = (prob * (grad_prob - centre)).astype(BF16)
    grad_q = jnp.einsum("lhqk,lkhd->lqhd", grad_scores, k, preferred_element_type=F32) * scale
    grad_k = jnp.einsum("lhqk,lqhd->lkhd", grad_scores, q, preferred_element_type=F32) * scale
    grad_v = jnp.einsum(
        "lhqk,lqhd->lkhd", prob.astype(BF16), grad, preferred_element_type=F32
    )
    return (grad_q, grad_k, grad_v)


def pair_sum(part):
    mine = lax.optimization_barrier(part.astype(BF16))
    return mine.astype(F32) + swap(mine, T).astype(F32)


def on_device(
    tokens,
    context,
    live_count,
    cotangent,
    triple_weight,
    attn_out_weight,
    cross_query_weight,
    cross_pair_weight,
    cross_out_weight,
    gate_up_weight,
    down_weight,
    norm_gains,
    norm_shifts,
):
    b = lax.axis_index("B")
    c = lax.axis_index("C")
    t = lax.axis_index(T)
    outer = lax.axis_size("A")
    slots, length, width = tokens.shape
    rows = slots * length
    half = rows // 2
    cond = context.shape[1]
    block = triple_weight.shape[0]
    local = triple_weight.shape[2]
    heads = local // HD
    units = gate_up_weight.shape[2]
    part_units = units // 2
    q_rows = width // 4

    def halves(w):
        k = w.shape[1]
        w = w.reshape(block, k, 2, part_units)
        own = pick(c, w[:, :, 0], w[:, :, 1]).reshape(block, k * part_units)
        other = pick(c, w[:, :, 1], w[:, :, 0]).reshape(block, k * part_units)
        return (own, other)

    gu_own, gu_other = halves(gate_up_weight)
    down_own, down_other = halves(down_weight.T.reshape(block, 1, units))
    norm_cols = jnp.concatenate([norm_gains, norm_shifts], axis=0).T
    norm_cols = jnp.pad(norm_cols, ((0, 0), (0, 128 - norm_cols.shape[1])))
    pack_one = jnp.concatenate(
        [triple_weight.reshape(block, 3 * local), attn_out_weight.T, norm_cols], axis=1
    )
    pack_two = jnp.concatenate(
        [
            jnp.concatenate([cross_query_weight, cross_out_weight.T], axis=1),
            cross_pair_weight.reshape(cross_pair_weight.shape[0], 2 * local),
        ],
        axis=0,
    )
    down_in = jnp.concatenate([down_own, swap(down_other, "C")], axis=1)
    gu_in = jnp.concatenate([gu_own, swap(gu_other, "C")], axis=1)
    z_one = gather_z(pack_one)
    z_two = gather_z(pack_two)
    z_down = gather_z(down_in)
    z_gu = gather_z(gu_in)
    w_one = gather_full(z_one)
    z_two = z_two.reshape(outer, pack_two.shape[0], 2 * local)
    w_two = gather_full(z_two[:, :block].reshape(outer * block, 2 * local))
    w_pair = gather_full(z_two[:, block:].reshape(-1, 2 * local))
    w_down = gather_half(z_down)
    w_gu = gather_half(z_gu)
    w_triple = w_one[:, : 3 * local]
    w_attn = w_one[:, 3 * local : 4 * local]
    norms = w_one[:, 4 * local : 4 * local + 6].T.astype(F32)
    w_cq = w_two[:, :local]
    w_cross = w_two[:, local:]

    live = (live_count[0] > jnp.arange(slots)).astype(F32)
    live_rows = jnp.repeat(live, length)[:, None]
    start = to_rel(tokens.reshape(rows, width), outer, b, c).astype(F32)
    grad_top = to_rel(cotangent.reshape(rows, width), outer, b, c).astype(F32) * live_rows
    ctx = to_rel(context.reshape(slots * cond, -1), outer, b, c)

    def by_core(value):
        return (
            pick(t, value[:half], value[half:]),
            pick(t, value[half:], value[:half]),
        )

    def from_core(mine, other):
        return jnp.concatenate([pick(t, mine, other), pick(t, other, mine)], axis=0)

    def spread(value):
        mine, other = by_core(value)
        far = flip_half(swap(mine, "C"))
        return jnp.concatenate([mine, other, far, swap(far, T)], axis=0)

    def collect(part):
        part = part.astype(BF16)
        send = jnp.concatenate([part[half : 2 * half], part[3 * half :]], axis=0)
        got = swap(send, T).astype(F32)
        near = part[:half].astype(F32) + got[:half]
        far = part[2 * half : 3 * half].astype(F32) + got[half:]
        return near + swap(flip_half(far.astype(BF16)), "C").astype(F32)

    grad_all = spread(grad_top.astype(BF16))

    cos_table, sin_table = rotary_tables(length)
    n1, hat_one, factor_one = norm_forward(start, norms[0], norms[3])
    raw = nn(n1, w_triple).reshape(slots, length, 3, heads, HD)
    q = rotate(raw[:, :, 0], cos_table, sin_table).astype(BF16)
    k = rotate(raw[:, :, 1], cos_table, sin_table).astype(BF16)
    v = raw[:, :, 2].astype(BF16)
    o1, logsum_one = attend(q, k, v)
    o1 = o1.reshape(rows, local)
    h1 = start + pair_sum(nt(o1, w_attn))
    n2, hat_two, factor_two = norm_forward(h1, norms[1], norms[4])
    cq = nn(n2, w_cq).astype(BF16).reshape(slots, length, heads, HD)
    pair = nn(ctx, w_pair).astype(BF16).reshape(slots, cond, 2, heads, HD)
    ck, cv = pair[:, :, 0], pair[:, :, 1]
    o2, logsum_two = attend(cq, ck, cv)
    o2 = o2.reshape(rows, local)
    h2 = h1 + pair_sum(nt(o2, w_cross))
    n3, hat_three, factor_three = norm_forward(h2, norms[2], norms[5])
    n3_all = spread(n3)
    gate = nn(n3_all, w_gu[:, :part_units])
    upper = nn(n3_all, w_gu[:, part_units:])
    sig = jax.nn.sigmoid(gate)
    silu = gate * sig
    hidden = (silu * upper).astype(BF16)

    g_down = scatter_half(grad_all, hidden)
    dhid = nn(grad_all, w_down)
    dgu = jnp.concatenate(
        [
            (dhid * upper * (sig * (1.0 + gate * (1.0 - sig)))).astype(BF16),
            (dhid * silu).astype(BF16),
        ],
        axis=1,
    )
    g_gu = scatter_half(n3_all, dgu)
    dn3 = collect(nt(dgu, w_gu)).astype(BF16)
    dn3 = lax.optimization_barrier(dn3)
    dn3 = from_core(dn3, swap(dn3, T)).astype(F32)
    back, gain_three, shift_three = norm_backward(dn3, hat_three, factor_three, norms[2])
    dh2 = grad_top + back

    out_half = collect(nt(hidden, w_down)) + by_core(h2)[0]
    out_half = (out_half * pick(t, live_rows[:half], live_rows[half:])).astype(BF16)
    out_half = lax.optimization_barrier(out_half)
    mixed = from_core(out_half, swap(out_half, T))

    dc = dh2.astype(BF16)
    g_cross = scatter_full(dc, o2)
    grad_o = nn(dc, w_cross).astype(BF16).reshape(slots, length, heads, HD)
    dcq, dck, dcv = attend_back(cq, ck, cv, grad_o, logsum_two)
    dcq = dcq.astype(BF16).reshape(rows, local)
    dpair = jnp.concatenate(
        [
            dck.astype(BF16).reshape(slots * cond, local),
            dcv.astype(BF16).reshape(slots * cond, local),
        ],
        axis=1,
    )
    g_cq = scatter_full(n2, dcq)
    g_pair = scatter_full(ctx, dpair)
    dn2 = pair_sum(nt(dcq, w_cq))
    dctx = pair_sum(nt(dpair, w_pair))
    back, gain_two, shift_two = norm_backward(dn2, hat_two, factor_two, norms[1])
    dh1 = dh2 + back

    da = dh1.astype(BF16)
    g_attn = scatter_full(da, o1)
    grad_o = nn(da, w_attn).astype(BF16).reshape(slots, length, heads, HD)
    dq, dk, dv = attend_back(q, k, v, grad_o, logsum_one)
    draw = jnp.concatenate(
        [
            rotate(dq, cos_table, -sin_table).astype(BF16).reshape(rows, local),
            rotate(dk, cos_table, -sin_table).astype(BF16).reshape(rows, local),
            dv.astype(BF16).reshape(rows, local),
        ],
        axis=1,
    )
    g_triple = scatter_full(n1, draw)
    dn1 = pair_sum(nt(draw, w_triple))
    back, gain_one, shift_one = norm_backward(dn1, hat_one, factor_one, norms[0])
    dtok = dh1 + back

    g_norm = jnp.stack([gain_one, gain_two, gain_three, shift_one, shift_two, shift_three], axis=1)
    g_norm = jnp.pad(g_norm, ((0, 0), (0, 128 - g_norm.shape[1])))
    sent = swap(g_norm[2 * q_rows :], "C")
    g_norm = g_norm[: 2 * q_rows] + sent
    sent = swap(g_norm[q_rows:], "B")
    g_norm = scatter_z(g_norm[:q_rows] + sent)

    def units_back(g, k):
        n = g.shape[1] // 2
        far = swap(g[:, n:], "C").reshape(block, k, part_units)
        own = g[:, :n].reshape(block, k, part_units)
        return jnp.concatenate([pick(c, own, far), pick(c, far, own)], axis=2).astype(F32)

    grad_gate_up = units_back(g_gu, 2)
    grad_down = units_back(g_down, 1).reshape(block, units).T

    return (
        from_rel(mixed, outer, b, c).reshape(tokens.shape),
        from_rel(dtok, outer, b, c).reshape(tokens.shape),
        from_rel(dctx, outer, b, c).reshape(context.shape),
        g_triple.astype(F32).reshape(block, 3, local),
        g_attn.astype(F32).T,
        g_cq.astype(F32),
        g_pair.astype(F32).reshape(-1, 2, local),
        g_cross.astype(F32).T,
        grad_gate_up,
        grad_down,
        g_norm[:, :3].T,
        g_norm[:, 3:6].T,
    )


def solution(mesh):
    dp, tensor = mesh.devices.shape
    inner = Mesh(mesh.devices.reshape(dp // 4, 2, 2, tensor), DP + (T,))
    rows_dp = P(DP, None, None)
    placed = (
        rows_dp,
        rows_dp,
        P(DP),
        rows_dp,
        P(DP, None, T),
        P(T, DP),
        P(DP, T),
        P(DP, None, T),
        P(T, DP),
        P(DP, None, T),
        P(T, DP),
        P(None, DP),
        P(None, DP),
    )
    return jax.shard_map(
        on_device,
        mesh=inner,
        in_specs=placed,
        out_specs=(
            rows_dp,
            rows_dp,
            rows_dp,
            P(DP, None, T),
            P(T, DP),
            P(DP, T),
            P(DP, None, T),
            P(T, DP),
            P(DP, None, T),
            P(T, DP),
            P(None, DP),
            P(None, DP),
        ),
        check_vma=False,
    )
```

```python
import functools

import jax
import jax.numpy as jnp
import numpy as np
from jax import lax
from jax.experimental import pallas as pl
from jax.experimental.pallas import tpu as pltpu
from jax.sharding import Mesh
from jax.sharding import PartitionSpec as P

HD = 64
ROT = 32
GROUP = 4
GW = GROUP * HD
UB = 256
EPSILON = 1e-05
SCALE = HD ** (-0.5)
F32 = jnp.float32
BF16 = jnp.bfloat16
DP = ("A", "B", "C")
T = "T"
FLIP = [(0, 1), (1, 0)]
AXIS = {"x": "C", "y": "B"}
VMEM_LIMIT = 58 * 1024 * 1024


class Lane:
    def __init__(self):
        self.last = None

    def run(self, move, value):
        if self.last is not None:
            value, _ = lax.optimization_barrier((value, self.last))
        self.last = move(value)
        return self.last


LANES = {}
TAIL = Lane()


def swap(value, axis):
    move = functools.partial(lax.ppermute, axis_name=axis, perm=FLIP)
    return LANES[axis].run(move, value) if axis in LANES else move(value)


def dot(left, right, dims):
    return lax.dot_general(left, right, (dims, ((), ())), preferred_element_type=F32)


def nn(left, right):
    return dot(left, right, ((1,), (0,)))


def nt(left, right):
    return dot(left, right, ((1,), (1,)))


def tn(left, right):
    return dot(left, right, ((0,), (0,)))


def pick(flag, when_zero, when_one):
    return jnp.where(flag == 0, when_zero, when_one)


def to_rel(values, outer, b, c):
    lead = values.shape[:-1]
    n = len(lead)
    v = values.reshape(lead + (outer, 2, 2, -1))
    v = jnp.transpose(v, tuple(range(n)) + (n + 2, n + 1, n, n + 3)).reshape(values.shape)
    return flip_blocks(v, b, c)


def flip_blocks(v, b, c):
    w = v.shape[-1]
    v = pick(c, v, jnp.concatenate([v[..., w // 2 :], v[..., : w // 2]], axis=-1))
    q = w // 4
    turned = [v[..., q : 2 * q], v[..., :q], v[..., 3 * q :], v[..., 2 * q : 3 * q]]
    return pick(b, v, jnp.concatenate(turned, axis=-1))


def from_rel(values, outer, b, c):
    lead = values.shape[:-1]
    n = len(lead)
    v = flip_blocks(values, b, c).reshape(lead + (2, 2, outer, -1))
    v = jnp.transpose(v, tuple(range(n)) + (n + 2, n + 1, n, n + 3))
    return v.reshape(values.shape)


def flip_half(values):
    half = values.shape[-1] // 2
    return jnp.concatenate([values[..., half:], values[..., :half]], axis=-1)


def gather_z(shard):
    return lax.all_gather(shard, "A", axis=0, tiled=True)


def scatter_z(rows):
    return lax.psum_scatter(rows, "A", scatter_dimension=0, tiled=True)


def hold(value, *others):
    return lax.optimization_barrier((value,) + others)[0]


def gather(shard, split):
    first = gather_z(shard)
    over_y, over_x = swap(first, "B"), swap(first, "C")
    fourth = []
    if split > 0:
        fourth.append((swap(over_y[:, :split], "C"), 0, split))
    if split < shard.shape[1]:
        fourth.append((swap(over_x[:, split:], "B"), split, shard.shape[1]))
    n = shard.shape[1]
    return {
        (0, 0): [(first, 0, n)],
        (0, 1): [(over_y, 0, n)],
        (1, 0): [(over_x, 0, n)],
        (1, 1): fourth,
    }


def columns(pieces, lo, width):
    found = []
    for p in PIECES:
        for a, begin, end in pieces[p]:
            if begin <= lo and lo + width <= end:
                found.append((a, (lo - begin) // width))
    return found


PIECES = ((0, 0), (0, 1), (1, 0), (1, 1))


class Scatter:
    def __init__(self, order):
        self.order = order

    def first(self, sent, kept):
        self.kept, self.got = kept, swap(sent, AXIS[self.order[0]])
        return self

    def second(self):
        n = self.kept.shape[1] // 2
        far = (self.kept[:, n:].astype(F32) + self.got[:, n:].astype(F32)).astype(BF16)
        moved = swap(far, AXIS[self.order[1]])
        near = self.kept[:, :n].astype(F32) + self.got[:, :n].astype(F32)
        self.kept = (near + moved.astype(F32)).astype(BF16)
        return self

    def third(self):
        return TAIL.run(scatter_z, self.kept).astype(F32)


def full(array):
    nd = array.ndim
    return pl.BlockSpec(array.shape, lambda *_: (0,) * nd)


def piece_specs(found, n):
    return [pl.BlockSpec((a.shape[0], n), functools.partial(lambda i, *_: (0, i), i)) for a, i in found]


def piece_args(found):
    return [a for a, _ in found]


def call(body, outs, ins, specs, out_specs, grid=(1,), scratch=(), flops=0, name=None):
    moved = sum(int(np.prod(o.shape)) * o.dtype.itemsize for o in outs)
    moved += sum(int(np.prod(i.shape)) * i.dtype.itemsize for i in ins)
    return pl.pallas_call(
        body,
        out_shape=outs,
        grid=grid,
        in_specs=specs,
        out_specs=out_specs,
        scratch_shapes=list(scratch),
        compiler_params=pltpu.CompilerParams(
            dimension_semantics=("arbitrary",) * len(grid), vmem_limit_bytes=VMEM_LIMIT
        ),
        cost_estimate=pl.CostEstimate(flops=1, transcendentals=0, bytes_accessed=1),
        name=name,
    )(*ins)


def shape(dims, dtype):
    return jax.ShapeDtypeStruct(dims, dtype)


def head_masks(value):
    lane = lax.broadcasted_iota(jnp.int32, (1, GW), 1) // HD
    return [jnp.where(lane == h, value, 0.0).astype(BF16) for h in range(GROUP)]


def probabilities(qm, k, bias):
    scores = nt(qm, k)
    if bias is not None:
        scores = scores + bias
    top = jnp.max(scores, axis=-1, keepdims=True)
    e = jnp.exp(scores - top)
    return e * (1.0 / jnp.sum(e, axis=-1, keepdims=True))


def attention(q, k, v, bias):
    out = None
    for m, s in zip(head_masks(1.0), head_masks(SCALE)):
        p = probabilities(q * s, k, bias).astype(BF16)
        o = nn(p, v * m)
        out = o if out is None else out + o
    return out


def attention_back(q, k, v, do, bias):
    dq = dk = dv = None
    for m, s in zip(head_masks(1.0), head_masks(SCALE)):
        qm = q * s
        p = probabilities(qm, k, bias)
        dom = do * m
        dp = nt(dom, v)
        centre = jnp.sum(p * dp, axis=-1, keepdims=True)
        ds = (p * (dp - centre)).astype(BF16)
        a, b, c = nn(ds, k * s), tn(ds, qm), tn(p.astype(BF16), dom)
        dq, dk, dv = (a, b, c) if dq is None else (dq + a, dk + b, dv + c)
    return (dq, dk, dv)


def turn(u, cos, sin_a, sin_b):
    return u * cos + pltpu.roll(u, GW - ROT // 2, 1) * sin_a + pltpu.roll(u, ROT // 2, 1) * sin_b


def rotary_tables(length):
    half_dim = ROT // 2
    freqs = 10000.0 ** (-(2.0 * jnp.arange(half_dim, dtype=F32) / ROT))
    angles = jnp.arange(length, dtype=F32)[:, None] * freqs[None, :]
    cos, sin = jnp.cos(angles), jnp.sin(angles)
    rest = jnp.zeros((length, HD - ROT), F32)
    none = jnp.zeros_like(sin)
    return tuple(
        jnp.tile(jnp.concatenate(parts, axis=1), (1, GROUP))
        for parts in ((cos, cos, rest + 1.0), (-sin, none, rest), (none, sin, rest))
    )


def norm_rows(pieces, at, outer_rows):
    found = columns(pieces, at, 128)

    def body(*refs):
        for i in range(4):
            refs[4][:, i * outer_rows : (i + 1) * outer_rows] = refs[i][...].astype(F32).T[:8, :]

    out = shape((8, 4 * outer_rows), F32)
    return call(body, [out], piece_args(found), piece_specs(found, 128), [full(out)], name="norm_rows")[0]


def restore(values, turned_b, turned_c, outer):
    rows, width = values.shape
    block = width // (4 * outer)
    h, q = width // 2, width // 4
    step = 128

    def body(b_ref, c_ref, v_ref, out_ref):
        v = v_ref[...]
        v = jnp.where(c_ref[0] == 0, v, jnp.concatenate([v[:, h:], v[:, :h]], axis=1))
        turned = [v[:, q : 2 * q], v[:, :q], v[:, 3 * q :], v[:, 2 * q : 3 * q]]
        v = jnp.where(b_ref[0] == 0, v, jnp.concatenate(turned, axis=1))
        out_ref[...] = jnp.concatenate(
            [
                v[:, (2 * c + b) * q + a * block : (2 * c + b) * q + (a + 1) * block]
                for a in range(outer)
                for b in range(2)
                for c in range(2)
            ],
            axis=1,
        )

    row = pl.BlockSpec((step, width), lambda i: (i, 0))
    flag = pl.BlockSpec(memory_space=pltpu.SMEM)
    return call(
        body,
        [shape((rows, width), values.dtype)],
        [turned_b.reshape(1), turned_c.reshape(1), values],
        [flag, flag, row],
        [row],
        grid=(rows // step,),
        name="restore",
    )[0]


def add_norm(base, mine, other, norms, index):
    rows, width = base.shape
    step = 256
    extra = [] if mine is None else [mine, other]

    def body(*refs):
        base_ref, norm_ref = refs[0], refs[1]
        h = base_ref[...].astype(F32)
        if extra:
            h = h + (refs[2][...].astype(F32) + refs[3][...].astype(F32))
        outs = refs[2 + len(extra) :]
        average = jnp.mean(h, axis=-1, keepdims=True)
        centred = h - average
        spread = jnp.mean(centred * centred, axis=-1, keepdims=True)
        normed = centred * lax.rsqrt(spread + EPSILON)
        gain = norm_ref[index : index + 1, :]
        shift = norm_ref[index + 3 : index + 4, :]
        outs[0][...] = (normed * gain + shift).astype(BF16)
        if extra:
            outs[1][...] = h

    row = pl.BlockSpec((step, width), lambda i: (i, 0))
    outs = [shape((rows, width), BF16)] + ([shape((rows, width), F32)] if extra else [])
    return call(
        body,
        outs,
        [base, norms] + extra,
        [row, full(norms)] + [row] * len(extra),
        [row] * len(outs),
        grid=(rows // step,),
        flops=rows * width * 12,
        name="add_norm",
    )


def norm_back(mine, other, h, above, norms, index):
    rows, width = h.shape
    step = 256

    def body(mine_ref, other_ref, h_ref, above_ref, norm_ref, out_ref, low_ref, sums_ref):
        dn = mine_ref[...].astype(F32) + other_ref[...].astype(F32)
        h = h_ref[...].astype(F32)
        average = jnp.mean(h, axis=-1, keepdims=True)
        centred = h - average
        spread = jnp.mean(centred * centred, axis=-1, keepdims=True)
        factor = lax.rsqrt(spread + EPSILON)
        normed = centred * factor
        scaled = dn * norm_ref[index : index + 1, :]
        first = jnp.mean(scaled, axis=-1, keepdims=True)
        second = jnp.mean(scaled * normed, axis=-1, keepdims=True)
        d = above_ref[...].astype(F32) + factor * (scaled - first - normed * second)
        out_ref[...] = d
        low_ref[...] = d.astype(BF16)

        @pl.when(pl.program_id(0) == 0)
        def _():
            sums_ref[...] = jnp.zeros_like(sums_ref)

        sums_ref[0:1, :] += jnp.sum(dn * normed, axis=0, keepdims=True)
        sums_ref[1:2, :] += jnp.sum(dn, axis=0, keepdims=True)

    row = pl.BlockSpec((step, width), lambda i: (i, 0))
    return call(
        body,
        [shape((rows, width), F32), shape((rows, width), BF16), shape((8, width), F32)],
        [mine, other, h, above, norms],
        [row, row, row, row, full(norms)],
        [row, row, pl.BlockSpec((8, width), lambda i: (0, 0))],
        grid=(rows // step,),
        flops=rows * width * 20,
        name="norm_back",
    )


def self_forward(n, pieces, tables, total, slots, last):
    rows, width = n.shape
    length = rows // slots
    q4 = width // 4
    cols = 4 * GW

    def body(*refs):
        n_ref, w_refs, tabs = refs[0], refs[1:5], refs[5:8]
        k = 8
        total_ref = None
        if total is not None:
            total_ref = refs[8]
            k = 9
        keep_ref, part_ref, w, raw = refs[k:]
        for i, r in enumerate(w_refs):
            w[i * q4 : (i + 1) * q4, :] = r[...]
        raw[...] = nn(n_ref[...], w[:, : 3 * GW])
        cos, sin_a, sin_b = (r[...] for r in tabs)
        for l in range(slots):
            at = slice(l * length, (l + 1) * length)
            q = turn(raw[at, :GW], cos, sin_a, sin_b).astype(BF16)
            key = turn(raw[at, GW : 2 * GW], cos, sin_a, sin_b).astype(BF16)
            v = raw[at, 2 * GW :].astype(BF16)
            keep_ref[at, :GW] = q
            keep_ref[at, GW : 2 * GW] = key
            keep_ref[at, 2 * GW : 3 * GW] = v
            keep_ref[at, 3 * GW :] = attention(q, key, v, None).astype(BF16)
        part = nt(keep_ref[:, 3 * GW :], w[:, 3 * GW :])
        if total_ref is not None:
            part = part + total_ref[...]
        part_ref[...] = part.astype(part_ref.dtype)

    ins = [n] + piece_args(pieces) + list(tables) + ([] if total is None else [total])
    specs = [full(n)] + piece_specs(pieces, cols) + [full(a) for a in tables]
    specs += [] if total is None else [full(total)]
    outs = [shape((rows, cols), BF16), shape((rows, width), BF16 if last else F32)]
    return call(
        body,
        outs,
        ins,
        specs,
        [full(o) for o in outs],
        scratch=[pltpu.VMEM((width, cols), BF16), pltpu.VMEM((rows, 3 * GW), F32)],
        flops=2 * rows * width * cols,
        name="self_forward",
    )


def load_cross(w_refs, w, wp, at, block, pair_block):
    both = block + pair_block
    outer = w_refs[0][0].shape[0] // both
    for i, parts in enumerate(w_refs):
        for o in range(outer):
            r = parts[0]
            w[(i * outer + o) * block : (i * outer + o + 1) * block, at] = r[o * both : o * both + block, :]
            wp[(i * outer + o) * pair_block : (i * outer + o + 1) * pair_block, at] = r[
                o * both + block : (o + 1) * both, :
            ]


def cross_operands(pieces, groups):
    found = [columns(pieces, j * 2 * GW, 2 * GW) for j in range(groups)]
    return [a for f in found for a in piece_args(f)], [q for f in found for q in piece_specs(f, 2 * GW)]


def cross_forward(n, ctx, pieces, slots, cond, groups, block, pair_block):
    rows, width = n.shape
    length, keys = rows // slots, ctx.shape[0] // slots
    cols = groups * 2 * GW

    def body(n_ref, ctx_ref, *refs):
        w_refs = refs[: 4 * groups]
        keep_ref, pair_ref, part_ref, w, wp, cq = refs[4 * groups :]
        lane = lax.broadcasted_iota(jnp.int32, (1, keys), 1)
        bias = jnp.where(lane < cond, 0.0, -1e30).astype(F32)
        part = None
        for j in range(groups):
            at_j = slice(2 * j * GW, 2 * (j + 1) * GW)
            load_cross([[r] for r in w_refs[4 * j : 4 * j + 4]], w, wp, at_j, block, pair_block)
            at_q = slice(2 * j * GW, (2 * j + 1) * GW)
            at_o = slice((2 * j + 1) * GW, (2 * j + 2) * GW)
            pair_ref[:, at_j] = nn(ctx_ref[...], wp[:, at_j]).astype(BF16)
            cq[...] = nn(n_ref[...], w[:, at_q]).astype(BF16)
            keep_ref[:, at_q] = cq[...]
            for l in range(slots):
                at = slice(l * length, (l + 1) * length)
                at_k = slice(l * keys, (l + 1) * keys)
                o = attention(cq[at, :], pair_ref[at_k, at_q], pair_ref[at_k, at_o], bias)
                keep_ref[at, at_o] = o.astype(BF16)
            more = nt(keep_ref[:, at_o], w[:, at_o])
            part = more if part is None else part + more
        part_ref[...] = part.astype(BF16)

    more_ins, more_specs = cross_operands(pieces, groups)
    ins = [n, ctx] + more_ins
    specs = [full(n), full(ctx)] + more_specs
    outs = [
        shape((rows, cols), BF16),
        shape((slots * keys, cols), BF16),
        shape((rows, width), BF16),
    ]
    return call(
        body,
        outs,
        ins,
        specs,
        [full(o) for o in outs],
        scratch=[
            pltpu.VMEM((width, cols), BF16),
            pltpu.VMEM((ctx.shape[1], cols), BF16),
            pltpu.VMEM((rows, GW), BF16),
        ],
        flops=2 * rows * width * cols + 2 * ctx.shape[0] * ctx.shape[1] * cols,
        name="cross_forward",
    )


def feed_forward(x, d, near_w, far_w, blocks):
    rows, width = x.shape
    q4 = width // 4
    cols = 6 * UB

    def body(x_ref, d_ref, a_ref, b_ref, keep_ref, send_ref, dn_ref, y_ref, w, dn, y):
        j = pl.program_id(0)
        for rx in range(2):
            for ry, r in enumerate((a_ref, b_ref)):
                at = (2 * rx + ry) * q4
                w[at : at + q4, :] = r[:, rx * 3 * UB : (rx + 1) * 3 * UB]
        gu = nn(x_ref[...], w[:, : 2 * UB])
        dh = nn(d_ref[...], w[:, 2 * UB :])
        gate, upper = gu[:, :UB], gu[:, UB:]
        sig = 1.0 / (1.0 + jnp.exp(-gate))
        silu = gate * sig
        hidden = (silu * upper).astype(BF16)
        dg = (dh * upper * (sig * (1.0 + gate * (1.0 - sig)))).astype(BF16)
        du = (dh * silu).astype(BF16)
        dgu = jnp.concatenate([dg, du], axis=1)
        for at, ref in ((0, keep_ref), (1, send_ref)):
            for rx in range(2):
                c0 = (2 * rx + at) * q4
                lo = rx * 3 * UB
                ref[:, lo : lo + 2 * UB] = tn(x_ref[:, c0 : c0 + q4], dgu).astype(BF16)
                ref[:, lo + 2 * UB : lo + 3 * UB] = tn(d_ref[:, c0 : c0 + q4], hidden).astype(BF16)
        more_dn = nt(dgu, w[:, : 2 * UB])
        more_y = nt(hidden, w[:, 2 * UB :])

        @pl.when(j == 0)
        def _():
            dn[...] = more_dn
            y[...] = more_y

        @pl.when(j > 0)
        def _():
            dn[...] += more_dn
            y[...] += more_y

        @pl.when(j == pl.num_programs(0) - 1)
        def _():
            dn_ref[...] = dn[...].astype(BF16)
            y_ref[...] = y[...].astype(BF16)

    block = pl.BlockSpec((q4, cols), lambda j: (0, j))
    from_w = [
        pl.BlockSpec((q4, cols), functools.partial(lambda i, j: (0, i + j), i * blocks))
        for _, i in (near_w, far_w)
    ]
    ins = [x, d, near_w[0], far_w[0]]
    outs = [shape((q4, blocks * cols), BF16)] * 2 + [shape((rows, width), BF16)] * 2
    return call(
        body,
        outs,
        ins,
        [full(x), full(d)] + from_w,
        [block, block] + [full(o) for o in outs[2:]],
        grid=(blocks,),
        scratch=[
            pltpu.VMEM((width, 3 * UB), BF16),
            pltpu.VMEM((rows, width), F32),
            pltpu.VMEM((rows, width), F32),
        ],
        flops=18 * rows * width * UB * blocks,
        name="feed_forward",
    )


def split_rows(left_ref, right, first, n, keep_ref, send_ref, lo=0, outer=1, at_row=0):
    q = left_ref.shape[1] // 4
    run = keep_ref.shape[0] // outer
    part = q // outer
    for rx, ry in PIECES:
        g = tn(left_ref[:, (2 * rx + ry) * q : (2 * rx + ry + 1) * q], right).astype(BF16)
        goes, other = (rx, ry) if first == "x" else (ry, rx)
        ref = send_ref if goes else keep_ref
        cols = slice(other * n + lo, other * n + lo + right.shape[1])
        for o in range(outer):
            ref[o * run + at_row : o * run + at_row + part, cols] = g[o * part : (o + 1) * part, :]


def cross_backward(dc, n, ctx, keep, pair_rows, pieces, slots, cond, groups, block, pair_block, first):
    rows, width = n.shape
    length, keys = rows // slots, ctx.shape[0] // slots
    cols = keep.shape[1]
    outer = width // 4 // block

    def body(dc_ref, n_ref, ctx_ref, keep_in, pair_in, *refs):
        w_refs = refs[: 4 * groups]
        g_keep, g_send, dn_ref, dctx_ref, w, wp, do, dcq, dpair = refs[4 * groups :]
        lane = lax.broadcasted_iota(jnp.int32, (1, keys), 1)
        bias = jnp.where(lane < cond, 0.0, -1e30).astype(F32)
        dn = None
        for j in range(groups):
            at_j = slice(2 * j * GW, 2 * (j + 1) * GW)
            load_cross([[r] for r in w_refs[4 * j : 4 * j + 4]], w, wp, at_j, block, pair_block)
            at_q = slice(2 * j * GW, (2 * j + 1) * GW)
            at_o = slice((2 * j + 1) * GW, (2 * j + 2) * GW)
            do[...] = nn(dc_ref[...], w[:, at_o]).astype(BF16)
            for l in range(slots):
                at = slice(l * length, (l + 1) * length)
                at_k = slice(l * keys, (l + 1) * keys)
                a, b, c = attention_back(
                    keep_in[at, at_q], pair_in[at_k, at_q], pair_in[at_k, at_o], do[at, :], bias
                )
                dcq[at, :] = a.astype(BF16)
                dpair[at_k, at_q] = b.astype(BF16)
                dpair[at_k, at_o] = c.astype(BF16)
            more = nt(dcq[...], w[:, at_q])
            dn = more if dn is None else dn + more
            split_rows(n_ref, dcq[...], first, cols, g_keep, g_send, 2 * j * GW, outer)
            split_rows(dc_ref, keep_in[:, at_o], first, cols, g_keep, g_send, (2 * j + 1) * GW, outer)
            split_rows(ctx_ref, dpair[:, at_j], first, cols, g_keep, g_send, 2 * j * GW, outer, block)
        dn_ref[...] = dn.astype(BF16)
        dctx_ref[...] = nt(dpair[...], wp[...]).astype(BF16)

    more_ins, more_specs = cross_operands(pieces, groups)
    ins = [dc, n, ctx, keep, pair_rows] + more_ins
    specs = [full(a) for a in ins[:5]] + more_specs
    grad_rows = outer * (block + pair_block)
    outs = [
        shape((grad_rows, 2 * cols), BF16),
        shape((grad_rows, 2 * cols), BF16),
        shape((rows, width), BF16),
        shape(ctx.shape, BF16),
    ]
    return call(
        body,
        outs,
        ins,
        specs,
        [full(o) for o in outs],
        scratch=[
            pltpu.VMEM((width, cols), BF16),
            pltpu.VMEM((ctx.shape[1], cols), BF16),
            pltpu.VMEM((rows, GW), BF16),
            pltpu.VMEM((rows, GW), BF16),
            pltpu.VMEM((slots * keys, cols), BF16),
        ],
        flops=4 * rows * width * cols + 4 * ctx.shape[0] * ctx.shape[1] * cols,
        name="cross_backward",
    )


def self_backward(da, n, keep, pieces, tables, total, slots, first, last):
    rows, width = n.shape
    length = rows // slots
    q4 = width // 4
    cols = 4 * GW

    def body(*refs):
        da_ref, n_ref, keep_in, w_refs, tabs = refs[0], refs[1], refs[2], refs[3:7], refs[7:10]
        k = 10
        total_ref = None
        if total is not None:
            total_ref = refs[10]
            k = 11
        g_keep, g_send, dn_ref, w, do, dt = refs[k:]
        for i, r in enumerate(w_refs):
            w[i * q4 : (i + 1) * q4, :] = r[...]
        do[...] = nn(da_ref[...], w[:, 3 * GW :]).astype(BF16)
        cos, sin_a, sin_b = (r[...] for r in tabs)
        for l in range(slots):
            at = slice(l * length, (l + 1) * length)
            dq, dk, dv = attention_back(
                keep_in[at, :GW], keep_in[at, GW : 2 * GW], keep_in[at, 2 * GW : 3 * GW], do[at, :], None
            )
            dt[at, :GW] = turn(dq, cos, -sin_a, -sin_b).astype(BF16)
            dt[at, GW : 2 * GW] = turn(dk, cos, -sin_a, -sin_b).astype(BF16)
            dt[at, 2 * GW :] = dv.astype(BF16)
        split_rows(n_ref, dt[...], first, cols, g_keep, g_send)
        split_rows(da_ref, keep_in[:, 3 * GW :], first, cols, g_keep, g_send, 3 * GW)
        dn = nt(dt[...], w[:, : 3 * GW])
        if total_ref is not None:
            dn = dn + total_ref[...]
        dn_ref[...] = dn.astype(dn_ref.dtype)

    ins = [da, n, keep] + piece_args(pieces) + list(tables) + ([] if total is None else [total])
    specs = [full(da), full(n), full(keep)] + piece_specs(pieces, cols)
    specs += [full(a) for a in tables] + ([] if total is None else [full(total)])
    outs = [
        shape((q4, 2 * cols), BF16),
        shape((q4, 2 * cols), BF16),
        shape((rows, width), BF16 if last else F32),
    ]
    return call(
        body,
        outs,
        ins,
        specs,
        [full(o) for o in outs],
        scratch=[
            pltpu.VMEM((width, cols), BF16),
            pltpu.VMEM((rows, GW), BF16),
            pltpu.VMEM((rows, 3 * GW), BF16),
        ],
        flops=4 * rows * width * cols,
        name="self_backward",
    )


ATTN_SPLIT = 2
CROSS_SPLIT = 1
FF_BLOCKS = (2, 2, 2)
FF_EARLY_Y = (True, False, False)
ATTN_SCATTER = ("xyz", "xyz", "yxz")
CROSS_SCATTER = "xyz"


def on_device(
    tokens,
    context,
    live_count,
    cotangent,
    triple_weight,
    attn_out_weight,
    cross_query_weight,
    cross_pair_weight,
    cross_out_weight,
    gate_up_weight,
    down_weight,
    norm_gains,
    norm_shifts,
):
    LANES.clear()
    TAIL.last = None
    LANES.update({name: Lane() for name in DP[1:]})
    b = lax.axis_index("B")
    c = lax.axis_index("C")
    t = lax.axis_index(T)
    outer = lax.axis_size("A")
    slots, length, width = tokens.shape
    rows = slots * length
    half = rows // 2
    cond = context.shape[1]
    keys = -(-cond // 16) * 16
    block = triple_weight.shape[0]
    pair_block = cross_pair_weight.shape[0]
    local = triple_weight.shape[2]
    groups = local // GW
    units = gate_up_weight.shape[2]
    part_blocks = units // 2 // UB
    q4 = width // 4

    def group(w, j):
        return w[..., j * GW : (j + 1) * GW]

    live = (live_count[0] > jnp.arange(slots)).astype(F32)
    live_rows = jnp.repeat(live, length)[:, None]

    def by_core(value):
        return (
            pick(t, value[:half], value[half:]),
            pick(t, value[half:], value[:half]),
        )

    def from_core(mine, other):
        return jnp.concatenate([pick(t, mine, other), pick(t, other, mine)], axis=0)

    def spread(value):
        mine, other = by_core(value)
        far = flip_half(swap(mine, "C"))
        return jnp.concatenate([mine, far, other, swap(far, T)], axis=0)

    def collect(parts):
        total = sum(p.astype(F32) for p in parts)
        got = total[:rows] + swap(total[rows:].astype(BF16), T).astype(F32)
        return got[:half] + swap(flip_half(got[half:].astype(BF16)), "C").astype(F32)

    attn_t, cross_t = attn_out_weight.T, cross_out_weight.T
    norm_in = jnp.concatenate([norm_gains, norm_shifts], axis=0).T
    attn_in = jnp.concatenate(
        [group(w, j) for j in range(groups) for w in [triple_weight[:, k] for k in range(3)] + [attn_t]]
        + [jnp.pad(norm_in, ((0, 0), (0, 128 - norm_in.shape[1])))],
        axis=1,
    )
    cross_in = jnp.concatenate(
        [
            jnp.concatenate(
                [group(w, j) for j in range(groups) for w in (cross_query_weight, cross_t)], axis=1
            ),
            jnp.concatenate(
                [group(cross_pair_weight[:, k], j) for j in range(groups) for k in range(2)], axis=1
            ),
        ],
        axis=0,
    )
    ff = jnp.concatenate([gate_up_weight, down_weight.T[:, None]], axis=1)
    ff = ff.reshape(block, 3, 2, part_blocks, UB).transpose(2, 0, 3, 1, 4)
    ff = ff.reshape(2, block, part_blocks, 3 * UB)
    ff_own = pick(c, ff[0], ff[1])
    ff_far = swap(pick(c, ff[1], ff[0]), "C")
    ff_in = jnp.stack([ff_own, ff_far], axis=2).reshape(block, part_blocks * 6 * UB)

    early = []
    at = 0
    for blocks, soon in zip(FF_BLOCKS, FF_EARLY_Y):
        shard = ff_in[:, at : at + blocks * 6 * UB]
        at += blocks * 6 * UB
        early.append((shard, swap(shard, "B") if soon else None))
    grad_top = to_rel(cotangent.reshape(rows, width), outer, b, c) * live_rows.astype(BF16)
    attn_w = gather(attn_in, ATTN_SPLIT * 4 * GW)
    cross_w = gather(cross_in, CROSS_SPLIT * 2 * GW)
    grad_all = spread(grad_top)
    norm_at = groups * 4 * GW
    norms = norm_rows(attn_w, norm_at, q4)
    ff_w = []
    for shard, moved in early:
        if moved is None:
            near = gather_z(shard)
            ff_w.append(((near, 0), (swap(near, "B"), 0)))
        else:
            whole = gather_z(jnp.concatenate([shard, moved], axis=1))
            ff_w.append(((whole, 0), (whole, 1)))

    start = to_rel(tokens.reshape(rows, width), outer, b, c)
    ctx = jnp.pad(to_rel(context, outer, b, c), ((0, 0), (0, keys - cond), (0, 0)))
    ctx = ctx.reshape(slots * keys, -1)
    tables = rotary_tables(length)

    (n1,) = add_norm(start, None, None, norms, 0)
    keep_one, part = [], None
    for j in range(groups):
        keep, part = self_forward(n1, columns(attn_w, j * 4 * GW, 4 * GW), tables, part, slots, j == groups - 1)
        keep_one.append(keep)
    part = hold(part, ff_w[0][0][0])
    n2, h1 = add_norm(start, part, swap(part, T), norms, 1)
    keep_two, pair_rows, part = cross_forward(n2, ctx, cross_w, slots, cond, groups, block, pair_block)
    part = hold(part, ff_w[1][0][0])
    n3, h2 = add_norm(h1, part, swap(part, T), norms, 2)
    n3_all = spread(n3)

    n3_all = hold(n3_all, *[w[0][0] for w in ff_w], ff_w[1][1][0])
    g_ff, dn3, y = [], [], []
    for i, blocks in enumerate(FF_BLOCKS):
        keep, send, dn_part, y_part = feed_forward(n3_all, grad_all, ff_w[i][0], ff_w[i][1], blocks)
        dn3.append(dn_part)
        y.append(y_part)
        g_ff.append((keep, lax.ppermute(send, "B", FLIP)))
    dn3 = collect(dn3).astype(BF16)
    dn3 = from_core(dn3, swap(dn3, T))

    def ff_sum(keep, got):
        return scatter_z((keep.astype(F32) + got.astype(F32)).astype(BF16))

    g_done = [ff_sum(hold(g_ff[0][0], dn3), g_ff[0][1])]

    dh2, dc, sums_three = norm_back(dn3, jnp.zeros_like(dn3), h2, grad_top, norms, 2)
    g_keep, g_send, dn2, dctx = cross_backward(
        dc, n2, ctx, keep_two, pair_rows, cross_w, slots, cond, groups, block, pair_block, CROSS_SCATTER[0]
    )
    g_cross = Scatter(CROSS_SCATTER).first(g_send, g_keep)
    dh1, da, sums_two = norm_back(dn2, swap(dn2, T), h1, dh2, norms, 1)
    g_done.append(ff_sum(hold(g_ff[1][0], da), g_ff[1][1]))
    g_attn, sends, dn1 = [], [], None
    for j in range(groups):
        g_keep, g_send, dn1 = self_backward(
            da,
            n1,
            keep_one[j],
            columns(attn_w, j * 4 * GW, 4 * GW),
            tables,
            dn1,
            slots,
            ATTN_SCATTER[j][0],
            j == groups - 1,
        )
        sends.append((g_send, g_keep))
    g_cross.kept = hold(g_cross.kept, dn1)
    g_cross.second()
    for j in range(groups):
        send, kept = sends[j]
        g_attn.append(Scatter(ATTN_SCATTER[j]).first(hold(send, dn1), kept))
    g_done.append(ff_sum(hold(g_ff[2][0], dn1), g_ff[2][1]))
    dn1 = hold(dn1, g_done[0])
    dtok, _, sums_one = norm_back(dn1, swap(dn1, T), start, dh1, norms, 0)
    dtok = restore(dtok, b, c, outer)

    sums = (sums_one, sums_two, sums_three)
    g_norm = jnp.concatenate([s[i : i + 1] for i in (0, 1) for s in sums], axis=0)
    g_norm = g_norm[:, : 2 * q4] + lax.ppermute(g_norm[:, 2 * q4 :], "C", FLIP)
    g_norm = g_norm[:, :q4] + lax.ppermute(g_norm[:, q4:], "B", FLIP)
    g_norm = TAIL.run(scatter_z, jnp.pad(g_norm.T, ((0, 0), (0, 128 - g_norm.shape[0]))))
    dctx = dctx.astype(F32) + swap(dctx, T).astype(F32)
    dctx = from_rel(dctx.reshape(slots, keys, -1)[:, :cond], outer, b, c)

    g_attn[0].second()
    g_attn[1].second()

    out_half = collect(y) + by_core(h2)[0]
    out_half = (out_half * pick(t, live_rows[:half], live_rows[half:])).astype(BF16)
    out_half = lax.optimization_barrier(out_half)
    mixed = restore(from_core(out_half, swap(out_half, T)), b, c, outer)

    g_attn[2].second()
    g_cross.kept = hold(g_cross.kept, *g_done)
    g_cross = g_cross.third()
    g_attn[0].kept = hold(g_attn[0].kept, dtok, dctx)
    g_attn_0 = g_attn[0].third()
    g_ff = jnp.concatenate(g_done, axis=1).reshape(block, part_blocks, 2, 3 * UB)
    own, far = g_ff[:, :, 0], lax.ppermute(g_ff[:, :, 1], "C", FLIP)
    g_ff = jnp.stack([pick(c, own, far), pick(c, far, own)], axis=1).astype(F32)
    g_ff = g_ff.reshape(block, 2, part_blocks, 3, UB).transpose(0, 3, 1, 2, 4)
    g_ff = g_ff.reshape(block, 3, units)
    g_gate_up, g_down = g_ff[:, :2], g_ff[:, 2].T
    g_attn[1].kept = hold(g_attn[1].kept, mixed, g_gate_up, g_down)
    g_attn = [g_attn_0] + [g.third() for g in g_attn[1:]]

    g_attn = jnp.stack([g.reshape(block, 4, GW) for g in g_attn], axis=2)
    g_attn = g_attn.reshape(block, 4, local)
    g_cross = g_cross.reshape(block + pair_block, groups, 2, GW)
    g_pair = g_cross[block:].transpose(0, 2, 1, 3)
    g_cross = g_cross[:block]

    return (
        mixed.reshape(tokens.shape),
        dtok.reshape(tokens.shape),
        dctx,
        g_attn[:, :3],
        g_attn[:, 3].T,
        g_cross[:, :, 0].reshape(block, local),
        g_pair.reshape(pair_block, 2, local),
        g_cross[:, :, 1].reshape(block, local).T,
        g_gate_up,
        g_down,
        g_norm[:, :3].T,
        g_norm[:, 3:6].T,
    )


def solution(mesh):
    dp, tensor = mesh.devices.shape
    inner = Mesh(mesh.devices.reshape(dp // 4, 2, 2, tensor), DP + (T,))
    rows_dp = P(DP, None, None)
    weights = (
        P(DP, None, T),
        P(T, DP),
        P(DP, T),
        P(DP, None, T),
        P(T, DP),
        P(DP, None, T),
        P(T, DP),
        P(None, DP),
        P(None, DP),
    )
    return jax.shard_map(
        on_device,
        mesh=inner,
        in_specs=(rows_dp, rows_dp, P(DP), rows_dp) + weights,
        out_specs=(rows_dp, rows_dp, rows_dp) + weights,
        check_vma=False,
    )
```

```python
import functools

import jax
import jax.numpy as jnp
import numpy as np
from jax import lax
from jax.experimental import pallas as pl
from jax.experimental.pallas import tpu as pltpu
from jax.sharding import Mesh
from jax.sharding import PartitionSpec as P

HD = 64
ROT = 32
GROUP = 4
GW = GROUP * HD
UB = 256
EPSILON = 1e-05
SCALE = HD ** (-0.5)
F32 = jnp.float32
BF16 = jnp.bfloat16
DP = ("A", "B", "C")
T = "T"
FLIP = [(0, 1), (1, 0)]
AXIS = {"x": "C", "y": "B"}
VMEM_LIMIT = 58 * 1024 * 1024


class Lane:
    def __init__(self):
        self.last = None

    def run(self, move, value):
        if self.last is not None:
            value, _ = lax.optimization_barrier((value, self.last))
        self.last = move(value)
        return self.last


LANES = {}
TAIL = Lane()


def swap(value, axis):
    move = functools.partial(lax.ppermute, axis_name=axis, perm=FLIP)
    return LANES[axis].run(move, value) if axis in LANES else move(value)


def dot(left, right, dims):
    return lax.dot_general(left, right, (dims, ((), ())), preferred_element_type=F32)


def nn(left, right):
    return dot(left, right, ((1,), (0,)))


def nt(left, right):
    return dot(left, right, ((1,), (1,)))


def tn(left, right):
    return dot(left, right, ((0,), (0,)))


def pick(flag, when_zero, when_one):
    return jnp.where(flag == 0, when_zero, when_one)


def to_rel(values, outer, b, c):
    lead = values.shape[:-1]
    n = len(lead)
    v = values.reshape(lead + (outer, 2, 2, -1))
    v = jnp.transpose(v, tuple(range(n)) + (n + 2, n + 1, n, n + 3)).reshape(values.shape)
    return flip_blocks(v, b, c)


def flip_blocks(v, b, c):
    w = v.shape[-1]
    v = pick(c, v, jnp.concatenate([v[..., w // 2 :], v[..., : w // 2]], axis=-1))
    q = w // 4
    turned = [v[..., q : 2 * q], v[..., :q], v[..., 3 * q :], v[..., 2 * q : 3 * q]]
    return pick(b, v, jnp.concatenate(turned, axis=-1))


def from_rel(values, outer, b, c):
    lead = values.shape[:-1]
    n = len(lead)
    v = flip_blocks(values, b, c).reshape(lead + (2, 2, outer, -1))
    v = jnp.transpose(v, tuple(range(n)) + (n + 2, n + 1, n, n + 3))
    return v.reshape(values.shape)


def flip_half(values):
    half = values.shape[-1] // 2
    return jnp.concatenate([values[..., half:], values[..., :half]], axis=-1)


def gather_z(shard):
    return lax.all_gather(shard, "A", axis=0, tiled=True)


def scatter_z(rows):
    return lax.psum_scatter(rows, "A", scatter_dimension=0, tiled=True)


def hold(value, *others):
    return lax.optimization_barrier((value,) + others)[0]


def gather(shard, split):
    first = gather_z(shard)
    over_y, over_x = swap(first, "B"), swap(first, "C")
    fourth = []
    if split > 0:
        fourth.append((swap(over_y[:, :split], "C"), 0, split))
    if split < shard.shape[1]:
        fourth.append((swap(over_x[:, split:], "B"), split, shard.shape[1]))
    n = shard.shape[1]
    return {
        (0, 0): [(first, 0, n)],
        (0, 1): [(over_y, 0, n)],
        (1, 0): [(over_x, 0, n)],
        (1, 1): fourth,
    }


def columns(pieces, lo, width):
    found = []
    for p in PIECES:
        for a, begin, end in pieces[p]:
            if begin <= lo and lo + width <= end:
                found.append((a, (lo - begin) // width))
    return found


PIECES = ((0, 0), (0, 1), (1, 0), (1, 1))


class Scatter:
    def __init__(self, order, grads):
        self.order, self.grads = order, grads

    def first_far(self):
        self.far = (self.grads[2], swap(self.grads[3], AXIS[self.order[0]]))
        return self

    def first_near(self):
        self.near = (self.grads[0], swap(self.grads[1], AXIS[self.order[0]]))
        return self

    def second(self):
        far = (self.far[0].astype(F32) + self.far[1].astype(F32)).astype(BF16)
        moved = swap(far, AXIS[self.order[1]])
        near = self.near[0].astype(F32) + self.near[1].astype(F32)
        self.kept = (near + moved.astype(F32)).astype(BF16)
        return self

    def third(self):
        return TAIL.run(scatter_z, self.kept).astype(F32)


def full(array):
    nd = array.ndim
    return pl.BlockSpec(array.shape, lambda *_: (0,) * nd)


def piece_specs(found, n):
    return [pl.BlockSpec((a.shape[0], n), functools.partial(lambda i, *_: (0, i), i)) for a, i in found]


def piece_args(found):
    return [a for a, _ in found]


def call(body, outs, ins, specs, out_specs, grid=(1,), scratch=(), flops=0, name=None):
    moved = sum(int(np.prod(o.shape)) * o.dtype.itemsize for o in outs)
    moved += sum(int(np.prod(i.shape)) * i.dtype.itemsize for i in ins)
    return pl.pallas_call(
        body,
        out_shape=outs,
        grid=grid,
        in_specs=specs,
        out_specs=out_specs,
        scratch_shapes=list(scratch),
        compiler_params=pltpu.CompilerParams(
            dimension_semantics=("arbitrary",) * len(grid), vmem_limit_bytes=VMEM_LIMIT
        ),
        cost_estimate=pl.CostEstimate(flops=1, transcendentals=0, bytes_accessed=1),
        name=name,
    )(*ins)


def shape(dims, dtype):
    return jax.ShapeDtypeStruct(dims, dtype)


def head_masks(value):
    lane = lax.broadcasted_iota(jnp.int32, (1, GW), 1) // HD
    return [jnp.where(lane == h, value, 0.0).astype(BF16) for h in range(GROUP)]


def probabilities(qm, k, bias):
    scores = nt(qm, k)
    if bias is not None:
        scores = scores + bias
    top = jnp.max(scores, axis=-1, keepdims=True)
    e = jnp.exp(scores - top)
    return e * (1.0 / jnp.sum(e, axis=-1, keepdims=True))


def attention(q, k, v, bias):
    out = None
    for m, s in zip(head_masks(1.0), head_masks(SCALE)):
        p = probabilities(q * s, k, bias).astype(BF16)
        o = nn(p, v * m)
        out = o if out is None else out + o
    return out


def attention_back(q, k, v, do, bias):
    dq = dk = dv = None
    for m, s in zip(head_masks(1.0), head_masks(SCALE)):
        qm = q * s
        p = probabilities(qm, k, bias)
        dom = do * m
        dp = nt(dom, v)
        centre = jnp.sum(p * dp, axis=-1, keepdims=True)
        ds = (p * (dp - centre)).astype(BF16)
        a, b, c = nn(ds, k * s), tn(ds, qm), tn(p.astype(BF16), dom)
        dq, dk, dv = (a, b, c) if dq is None else (dq + a, dk + b, dv + c)
    return (dq, dk, dv)


def turn(u, cos, sin_a, sin_b):
    return u * cos + pltpu.roll(u, GW - ROT // 2, 1) * sin_a + pltpu.roll(u, ROT // 2, 1) * sin_b


def rotary_tables(length):
    half_dim = ROT // 2
    freqs = 10000.0 ** (-(2.0 * jnp.arange(half_dim, dtype=F32) / ROT))
    angles = jnp.arange(length, dtype=F32)[:, None] * freqs[None, :]
    cos, sin = jnp.cos(angles), jnp.sin(angles)
    rest = jnp.zeros((length, HD - ROT), F32)
    none = jnp.zeros_like(sin)
    return tuple(
        jnp.tile(jnp.concatenate(parts, axis=1), (1, GROUP))
        for parts in ((cos, cos, rest + 1.0), (-sin, none, rest), (none, sin, rest))
    )


def norm_rows(pieces, at, outer_rows):
    found = columns(pieces, at, 128)

    def body(*refs):
        for i in range(4):
            refs[4][:, i * outer_rows : (i + 1) * outer_rows] = refs[i][...].astype(F32).T[:8, :]

    out = shape((8, 4 * outer_rows), F32)
    return call(body, [out], piece_args(found), piece_specs(found, 128), [full(out)], name="norm_rows")[0]


def restore(values, turned_b, turned_c, outer):
    rows, width = values.shape
    block = width // (4 * outer)
    h, q = width // 2, width // 4
    step = 128

    def body(b_ref, c_ref, v_ref, out_ref):
        v = v_ref[...]
        v = jnp.where(c_ref[0] == 0, v, jnp.concatenate([v[:, h:], v[:, :h]], axis=1))
        turned = [v[:, q : 2 * q], v[:, :q], v[:, 3 * q :], v[:, 2 * q : 3 * q]]
        v = jnp.where(b_ref[0] == 0, v, jnp.concatenate(turned, axis=1))
        out_ref[...] = jnp.concatenate(
            [
                v[:, (2 * c + b) * q + a * block : (2 * c + b) * q + (a + 1) * block]
                for a in range(outer)
                for b in range(2)
                for c in range(2)
            ],
            axis=1,
        )

    row = pl.BlockSpec((step, width), lambda i: (i, 0))
    flag = pl.BlockSpec(memory_space=pltpu.SMEM)
    return call(
        body,
        [shape((rows, width), values.dtype)],
        [turned_b.reshape(1), turned_c.reshape(1), values],
        [flag, flag, row],
        [row],
        grid=(rows // step,),
        name="restore",
    )[0]


def add_norm(base, mine, other, norms, index):
    rows, width = base.shape
    step = 256
    extra = [] if mine is None else [mine, other]

    def body(*refs):
        base_ref, norm_ref = refs[0], refs[1]
        h = base_ref[...].astype(F32)
        if extra:
            h = h + (refs[2][...].astype(F32) + refs[3][...].astype(F32))
        outs = refs[2 + len(extra) :]
        average = jnp.mean(h, axis=-1, keepdims=True)
        centred = h - average
        spread = jnp.mean(centred * centred, axis=-1, keepdims=True)
        normed = centred * lax.rsqrt(spread + EPSILON)
        gain = norm_ref[index : index + 1, :]
        shift = norm_ref[index + 3 : index + 4, :]
        outs[0][...] = (normed * gain + shift).astype(BF16)
        if extra:
            outs[1][...] = h

    row = pl.BlockSpec((step, width), lambda i: (i, 0))
    outs = [shape((rows, width), BF16)] + ([shape((rows, width), F32)] if extra else [])
    return call(
        body,
        outs,
        [base, norms] + extra,
        [row, full(norms)] + [row] * len(extra),
        [row] * len(outs),
        grid=(rows // step,),
        flops=rows * width * 12,
        name="add_norm",
    )


def norm_back(mine, other, h, above, norms, index):
    rows, width = h.shape
    step = 256

    def body(mine_ref, other_ref, h_ref, above_ref, norm_ref, out_ref, low_ref, sums_ref):
        dn = mine_ref[...].astype(F32) + other_ref[...].astype(F32)
        h = h_ref[...].astype(F32)
        average = jnp.mean(h, axis=-1, keepdims=True)
        centred = h - average
        spread = jnp.mean(centred * centred, axis=-1, keepdims=True)
        factor = lax.rsqrt(spread + EPSILON)
        normed = centred * factor
        scaled = dn * norm_ref[index : index + 1, :]
        first = jnp.mean(scaled, axis=-1, keepdims=True)
        second = jnp.mean(scaled * normed, axis=-1, keepdims=True)
        d = above_ref[...].astype(F32) + factor * (scaled - first - normed * second)
        out_ref[...] = d
        low_ref[...] = d.astype(BF16)

        @pl.when(pl.program_id(0) == 0)
        def _():
            sums_ref[...] = jnp.zeros_like(sums_ref)

        sums_ref[0:1, :] += jnp.sum(dn * normed, axis=0, keepdims=True)
        sums_ref[1:2, :] += jnp.sum(dn, axis=0, keepdims=True)

    row = pl.BlockSpec((step, width), lambda i: (i, 0))
    return call(
        body,
        [shape((rows, width), F32), shape((rows, width), BF16), shape((8, width), F32)],
        [mine, other, h, above, norms],
        [row, row, row, row, full(norms)],
        [row, row, pl.BlockSpec((8, width), lambda i: (0, 0))],
        grid=(rows // step,),
        flops=rows * width * 20,
        name="norm_back",
    )


def grouped_specs(pieces, n):
    out = []
    for p in PIECES:
        for a, begin, end in pieces[p]:
            lo, count = begin // n, (end - begin) // n
            pick_block = functools.partial(
                lambda lo, count, j: (0, jnp.clip(j - lo, 0, count - 1)), lo, count
            )
            out.append((a, pl.BlockSpec((a.shape[0], n), pick_block), lo, lo + count))
    return out


def load_grouped(found, refs, w, rows):
    j = pl.program_id(0)
    at = -rows
    for (_, _, lo, hi), r in zip(found, refs):
        if lo == 0:
            at += rows
        target = slice(at, at + rows)

        @pl.when((j >= lo) & (j < hi))
        def _(r=r, target=target):
            w[target, :] = r[...]


def constant(array):
    nd = array.ndim
    return pl.BlockSpec(array.shape, lambda *_: (0,) * nd, pipeline_mode=pl.Buffered(1))


def self_forward(n, pieces, tables, slots, groups):
    rows, width = n.shape
    length = rows // slots
    q4 = width // 4
    cols = 4 * GW
    found = grouped_specs(pieces, cols)

    def body(*refs):
        n_ref, w_refs, tabs = refs[0], refs[1 : 1 + len(found)], refs[1 + len(found) : 4 + len(found)]
        keep_ref, part_ref, w, raw, total = refs[4 + len(found) :]
        j = pl.program_id(0)
        load_grouped(found, w_refs, w, q4)
        raw[...] = nn(n_ref[...], w[:, : 3 * GW])
        cos, sin_a, sin_b = (r[...] for r in tabs)
        for l in range(slots):
            at = slice(l * length, (l + 1) * length)
            q = turn(raw[at, :GW], cos, sin_a, sin_b).astype(BF16)
            key = turn(raw[at, GW : 2 * GW], cos, sin_a, sin_b).astype(BF16)
            v = raw[at, 2 * GW :].astype(BF16)
            keep_ref[at, :GW] = q
            keep_ref[at, GW : 2 * GW] = key
            keep_ref[at, 2 * GW : 3 * GW] = v
            keep_ref[at, 3 * GW :] = attention(q, key, v, None).astype(BF16)
        part = nt(keep_ref[:, 3 * GW :], w[:, 3 * GW :])

        @pl.when(j == 0)
        def _():
            total[...] = part

        @pl.when(j > 0)
        def _():
            total[...] += part

        @pl.when(j == pl.num_programs(0) - 1)
        def _():
            part_ref[...] = total[...].astype(BF16)

    ins = [n] + [f[0] for f in found] + list(tables)
    specs = [constant(n)] + [f[1] for f in found] + [constant(a) for a in tables]
    outs = [shape((rows, groups * cols), BF16), shape((rows, width), BF16)]
    return call(
        body,
        outs,
        ins,
        specs,
        [pl.BlockSpec((rows, cols), lambda j: (0, j)), full(outs[1])],
        grid=(groups,),
        scratch=[
            pltpu.VMEM((width, cols), BF16),
            pltpu.VMEM((rows, 3 * GW), F32),
            pltpu.VMEM((rows, width), F32),
        ],
        name="self_forward",
    )


def load_cross(w_refs, w, wp, at, block, pair_block):
    both = block + pair_block
    outer = w_refs[0][0].shape[0] // both
    for i, parts in enumerate(w_refs):
        for o in range(outer):
            r = parts[0]
            w[(i * outer + o) * block : (i * outer + o + 1) * block, at] = r[o * both : o * both + block, :]
            wp[(i * outer + o) * pair_block : (i * outer + o + 1) * pair_block, at] = r[
                o * both + block : (o + 1) * both, :
            ]


def cross_operands(pieces, groups):
    found = [columns(pieces, j * 2 * GW, 2 * GW) for j in range(groups)]
    return [a for f in found for a in piece_args(f)], [q for f in found for q in piece_specs(f, 2 * GW)]


def cross_forward(n, ctx, pieces, slots, cond, groups, block, pair_block):
    rows, width = n.shape
    length, keys = rows // slots, ctx.shape[0] // slots
    cols = groups * 2 * GW

    def body(n_ref, ctx_ref, *refs):
        w_refs = refs[: 4 * groups]
        keep_ref, pair_ref, part_ref, w, wp, cq = refs[4 * groups :]
        lane = lax.broadcasted_iota(jnp.int32, (1, keys), 1)
        bias = jnp.where(lane < cond, 0.0, -1e30).astype(F32)
        part = None
        for j in range(groups):
            at_j = slice(2 * j * GW, 2 * (j + 1) * GW)
            load_cross([[r] for r in w_refs[4 * j : 4 * j + 4]], w, wp, at_j, block, pair_block)
            at_q = slice(2 * j * GW, (2 * j + 1) * GW)
            at_o = slice((2 * j + 1) * GW, (2 * j + 2) * GW)
            pair_ref[:, at_j] = nn(ctx_ref[...], wp[:, at_j]).astype(BF16)
            cq[...] = nn(n_ref[...], w[:, at_q]).astype(BF16)
            keep_ref[:, at_q] = cq[...]
            for l in range(slots):
                at = slice(l * length, (l + 1) * length)
                at_k = slice(l * keys, (l + 1) * keys)
                o = attention(cq[at, :], pair_ref[at_k, at_q], pair_ref[at_k, at_o], bias)
                keep_ref[at, at_o] = o.astype(BF16)
            more = nt(keep_ref[:, at_o], w[:, at_o])
            part = more if part is None else part + more
        part_ref[...] = part.astype(BF16)

    more_ins, more_specs = cross_operands(pieces, groups)
    ins = [n, ctx] + more_ins
    specs = [full(n), full(ctx)] + more_specs
    outs = [
        shape((rows, cols), BF16),
        shape((slots * keys, cols), BF16),
        shape((rows, width), BF16),
    ]
    return call(
        body,
        outs,
        ins,
        specs,
        [full(o) for o in outs],
        scratch=[
            pltpu.VMEM((width, cols), BF16),
            pltpu.VMEM((ctx.shape[1], cols), BF16),
            pltpu.VMEM((rows, GW), BF16),
        ],
        flops=2 * rows * width * cols + 2 * ctx.shape[0] * ctx.shape[1] * cols,
        name="cross_forward",
    )


def feed_forward(x, d, near_w, far_w, blocks, joint):
    rows, width = x.shape
    q4 = width // 4
    cols = 6 * UB

    def body(*refs):
        if not joint:
            x_ref, d_ref, a_ref, b_ref, keep_ref, send_ref, dn_ref, y_ref, w, dn, y = refs
        else:
            x_ref, d_ref, a_ref, b_ref, keep_ref, dn_ref, y_ref, w, dn, y = refs
        j = pl.program_id(0)
        for rx in range(2):
            for ry, r in enumerate((a_ref, b_ref)):
                at = (2 * rx + ry) * q4
                w[at : at + q4, :] = r[:, rx * 3 * UB : (rx + 1) * 3 * UB]
        gu = nn(x_ref[...], w[:, : 2 * UB])
        dh = nn(d_ref[...], w[:, 2 * UB :])
        gate, upper = gu[:, :UB], gu[:, UB:]
        sig = 1.0 / (1.0 + jnp.exp(-gate))
        silu = gate * sig
        hidden = (silu * upper).astype(BF16)
        dg = (dh * upper * (sig * (1.0 + gate * (1.0 - sig)))).astype(BF16)
        du = (dh * silu).astype(BF16)
        dgu = jnp.concatenate([dg, du], axis=1)
        for rx in range(2):
            for ref, right, lo, n in ((x_ref, dgu, 0, 2 * UB), (d_ref, hidden, 2 * UB, UB)):
                c0 = 2 * rx * q4
                at = slice(rx * 3 * UB + lo, rx * 3 * UB + lo + n)
                near = tn(ref[:, c0 : c0 + q4], right)
                far = tn(ref[:, c0 + q4 : c0 + 2 * q4], right)
                keep_ref[:, at] = near.astype(BF16)
                if joint:
                    keep_ref[:, cols + at.start : cols + at.stop] = far.astype(BF16)
                else:
                    send_ref[:, at] = far.astype(BF16)
        more_dn = nt(dgu, w[:, : 2 * UB])
        more_y = nt(hidden, w[:, 2 * UB :])

        @pl.when(j == 0)
        def _():
            dn[...] = more_dn
            y[...] = more_y

        @pl.when(j > 0)
        def _():
            dn[...] += more_dn
            y[...] += more_y

        @pl.when(j == pl.num_programs(0) - 1)
        def _():
            dn_ref[...] = dn[...].astype(BF16)
            y_ref[...] = y[...].astype(BF16)

    block = pl.BlockSpec((q4, cols), lambda j: (0, j))
    from_w = [
        pl.BlockSpec((q4, cols), functools.partial(lambda i, j: (0, i + j), i * blocks))
        for _, i in (near_w, far_w)
    ]
    ins = [x, d, near_w[0], far_w[0]]
    specs = [constant(x), constant(d)] + from_w
    if joint:
        outs = [shape((q4, 2 * blocks * cols), BF16)]
        out_specs = [pl.BlockSpec((q4, 2 * cols), lambda j: (0, j))]
    else:
        outs = [shape((q4, blocks * cols), BF16)] * 2
        out_specs = [block, block]
    sums = [shape((rows, width), BF16)] * 2
    return call(
        body,
        outs + sums,
        ins,
        specs,
        out_specs + [full(o) for o in sums],
        grid=(blocks,),
        scratch=[
            pltpu.VMEM((width, 3 * UB), BF16),
            pltpu.VMEM((rows, width), F32),
            pltpu.VMEM((rows, width), F32),
        ],
        flops=18 * rows * width * UB * blocks,
        name="feed_forward",
    )


def split_rows(left_ref, right, first, grads, cols, outer=1, at_row=0):
    q = left_ref.shape[1] // 4
    run = grads[0].shape[0] // outer
    part = q // outer
    for rx, ry in PIECES:
        g = tn(left_ref[:, (2 * rx + ry) * q : (2 * rx + ry + 1) * q], right).astype(BF16)
        goes, other = (rx, ry) if first == "x" else (ry, rx)
        for o in range(outer):
            grads[2 * other + goes][o * run + at_row : o * run + at_row + part, cols] = g[
                o * part : (o + 1) * part, :
            ]


def cross_backward(dc, n, ctx, keep, pair_rows, pieces, slots, cond, groups, block, pair_block, first):
    rows, width = n.shape
    length, keys = rows // slots, ctx.shape[0] // slots
    cols = keep.shape[1]
    outer = width // 4 // block

    def body(dc_ref, n_ref, ctx_ref, keep_in, pair_in, *refs):
        w_refs = refs[: 4 * groups]
        grads, (dn_ref, dctx_ref, w, wp, do, dcq, dpair) = refs[4 * groups : 4 * groups + 4], refs[4 * groups + 4 :]
        lane = lax.broadcasted_iota(jnp.int32, (1, keys), 1)
        bias = jnp.where(lane < cond, 0.0, -1e30).astype(F32)
        dn = None
        for j in range(groups):
            at_j = slice(2 * j * GW, 2 * (j + 1) * GW)
            load_cross([[r] for r in w_refs[4 * j : 4 * j + 4]], w, wp, at_j, block, pair_block)
            at_q = slice(2 * j * GW, (2 * j + 1) * GW)
            at_o = slice((2 * j + 1) * GW, (2 * j + 2) * GW)
            do[...] = nn(dc_ref[...], w[:, at_o]).astype(BF16)
            for l in range(slots):
                at = slice(l * length, (l + 1) * length)
                at_k = slice(l * keys, (l + 1) * keys)
                a, b, c = attention_back(
                    keep_in[at, at_q], pair_in[at_k, at_q], pair_in[at_k, at_o], do[at, :], bias
                )
                dcq[at, :] = a.astype(BF16)
                dpair[at_k, at_q] = b.astype(BF16)
                dpair[at_k, at_o] = c.astype(BF16)
            more = nt(dcq[...], w[:, at_q])
            dn = more if dn is None else dn + more
            split_rows(n_ref, dcq[...], first, grads, at_q, outer)
            split_rows(dc_ref, keep_in[:, at_o], first, grads, at_o, outer)
            split_rows(ctx_ref, dpair[:, at_j], first, grads, at_j, outer, block)
        dn_ref[...] = dn.astype(BF16)
        dctx_ref[...] = nt(dpair[...], wp[...]).astype(BF16)

    more_ins, more_specs = cross_operands(pieces, groups)
    ins = [dc, n, ctx, keep, pair_rows] + more_ins
    specs = [full(a) for a in ins[:5]] + more_specs
    grad_rows = outer * (block + pair_block)
    outs = [shape((grad_rows, cols), BF16)] * 4 + [shape((rows, width), BF16), shape(ctx.shape, BF16)]
    return call(
        body,
        outs,
        ins,
        specs,
        [full(o) for o in outs],
        scratch=[
            pltpu.VMEM((width, cols), BF16),
            pltpu.VMEM((ctx.shape[1], cols), BF16),
            pltpu.VMEM((rows, GW), BF16),
            pltpu.VMEM((rows, GW), BF16),
            pltpu.VMEM((slots * keys, cols), BF16),
        ],
        flops=4 * rows * width * cols + 4 * ctx.shape[0] * ctx.shape[1] * cols,
        name="cross_backward",
    )


def self_backward(da, n, keep, pieces, tables, slots, groups, firsts):
    rows, width = n.shape
    length = rows // slots
    q4 = width // 4
    cols = 4 * GW
    found = grouped_specs(pieces, cols)

    def body(*refs):
        da_ref, n_ref, keep_in = refs[:3]
        w_refs, tabs = refs[3 : 3 + len(found)], refs[3 + len(found) : 6 + len(found)]
        grads = [refs[6 + len(found) : 10 + len(found)], refs[10 + len(found) : 14 + len(found)]]
        dn_ref, w, do, dt, total = refs[14 + len(found) :]
        j = pl.program_id(0)
        load_grouped(found, w_refs, w, q4)
        do[...] = nn(da_ref[...], w[:, 3 * GW :]).astype(BF16)
        cos, sin_a, sin_b = (r[...] for r in tabs)
        for l in range(slots):
            at = slice(l * length, (l + 1) * length)
            dq, dk, dv = attention_back(
                keep_in[at, :GW], keep_in[at, GW : 2 * GW], keep_in[at, 2 * GW : 3 * GW], do[at, :], None
            )
            dt[at, :GW] = turn(dq, cos, -sin_a, -sin_b).astype(BF16)
            dt[at, GW : 2 * GW] = turn(dk, cos, -sin_a, -sin_b).astype(BF16)
            dt[at, 2 * GW :] = dv.astype(BF16)
        split_rows(n_ref, dt[:, : 2 * GW], firsts[0], grads[0], slice(0, 2 * GW))
        split_rows(n_ref, dt[:, 2 * GW :], firsts[1], grads[1], slice(0, GW))
        split_rows(da_ref, keep_in[:, 3 * GW :], firsts[1], grads[1], slice(GW, 2 * GW))
        dn = nt(dt[...], w[:, : 3 * GW])

        @pl.when(j == 0)
        def _():
            total[...] = dn

        @pl.when(j > 0)
        def _():
            total[...] += dn

        @pl.when(j == pl.num_programs(0) - 1)
        def _():
            dn_ref[...] = total[...].astype(BF16)

    ins = [da, n, keep] + [f[0] for f in found] + list(tables)
    step = pl.BlockSpec((rows, cols), lambda j: (0, j))
    specs = [constant(da), constant(n), step] + [f[1] for f in found] + [constant(a) for a in tables]
    outs = [shape((q4, groups * cols // 2), BF16)] * 8 + [shape((rows, width), BF16)]
    grad = pl.BlockSpec((q4, cols // 2), lambda j: (0, j))
    return call(
        body,
        outs,
        ins,
        specs,
        [grad] * 8 + [full(outs[8])],
        grid=(groups,),
        scratch=[
            pltpu.VMEM((width, cols), BF16),
            pltpu.VMEM((rows, GW), BF16),
            pltpu.VMEM((rows, 3 * GW), BF16),
            pltpu.VMEM((rows, width), F32),
        ],
        name="self_backward",
    )


ATTN_SPLIT = 2
CROSS_SPLIT = 1
FF_BLOCKS = (2, 2, 2)
FF_EARLY_Y = (True, False, False)
FF_JOINT = (True, True, False)
ATTN_SCATTER = ("yxz", "xyz")
CROSS_SCATTER = "xyz"


def on_device(
    tokens,
    context,
    live_count,
    cotangent,
    triple_weight,
    attn_out_weight,
    cross_query_weight,
    cross_pair_weight,
    cross_out_weight,
    gate_up_weight,
    down_weight,
    norm_gains,
    norm_shifts,
):
    LANES.clear()
    TAIL.last = None
    LANES.update({name: Lane() for name in DP[1:]})
    b = lax.axis_index("B")
    c = lax.axis_index("C")
    t = lax.axis_index(T)
    outer = lax.axis_size("A")
    slots, length, width = tokens.shape
    rows = slots * length
    half = rows // 2
    cond = context.shape[1]
    keys = -(-cond // 16) * 16
    block = triple_weight.shape[0]
    pair_block = cross_pair_weight.shape[0]
    local = triple_weight.shape[2]
    groups = local // GW
    units = gate_up_weight.shape[2]
    part_blocks = units // 2 // UB
    q4 = width // 4

    def group(w, j):
        return w[..., j * GW : (j + 1) * GW]

    live = (live_count[0] > jnp.arange(slots)).astype(F32)
    live_rows = jnp.repeat(live, length)[:, None]

    def by_core(value):
        return (
            pick(t, value[:half], value[half:]),
            pick(t, value[half:], value[:half]),
        )

    def from_core(mine, other):
        return jnp.concatenate([pick(t, mine, other), pick(t, other, mine)], axis=0)

    def spread(value, *others):
        mine, other = by_core(value)
        far = flip_half(swap(mine, "C"))
        if others:
            far = hold(far, *others)
        return jnp.concatenate([mine, far, other, swap(far, T)], axis=0)

    def collect(parts):
        total = sum(p.astype(F32) for p in parts)
        got = total[:rows] + swap(total[rows:].astype(BF16), T).astype(F32)
        return got[:half] + swap(flip_half(got[half:].astype(BF16)), "C").astype(F32)

    attn_t, cross_t = attn_out_weight.T, cross_out_weight.T
    norm_in = jnp.concatenate([norm_gains, norm_shifts], axis=0).T
    attn_in = jnp.concatenate(
        [group(w, j) for j in range(groups) for w in [triple_weight[:, k] for k in range(3)] + [attn_t]]
        + [jnp.pad(norm_in, ((0, 0), (0, 128 - norm_in.shape[1])))],
        axis=1,
    )
    cross_in = jnp.concatenate(
        [
            jnp.concatenate(
                [group(w, j) for j in range(groups) for w in (cross_query_weight, cross_t)], axis=1
            ),
            jnp.concatenate(
                [group(cross_pair_weight[:, k], j) for j in range(groups) for k in range(2)], axis=1
            ),
        ],
        axis=0,
    )
    ff = jnp.concatenate([gate_up_weight, down_weight.T[:, None]], axis=1)
    ff = ff.reshape(block, 3, 2, part_blocks, UB).transpose(2, 0, 3, 1, 4)
    ff = ff.reshape(2, block, part_blocks, 3 * UB)
    ff_own = pick(c, ff[0], ff[1])
    ff_far = swap(pick(c, ff[1], ff[0]), "C")
    ff_in = jnp.stack([ff_own, ff_far], axis=2).reshape(block, part_blocks * 6 * UB)

    early = []
    at = 0
    for blocks, soon in zip(FF_BLOCKS, FF_EARLY_Y):
        shard = ff_in[:, at : at + blocks * 6 * UB]
        at += blocks * 6 * UB
        early.append((shard, swap(shard, "B") if soon else None))
    grad_top = to_rel(cotangent.reshape(rows, width), outer, b, c) * live_rows.astype(BF16)
    attn_w = gather(attn_in, ATTN_SPLIT * 4 * GW)
    cross_w = gather(cross_in, CROSS_SPLIT * 2 * GW)
    grad_all = spread(grad_top)
    norm_at = groups * 4 * GW
    norms = norm_rows(attn_w, norm_at, q4)
    ff_w = []
    for shard, moved in early:
        if moved is None:
            near = gather_z(shard)
            ff_w.append(((near, 0), (swap(near, "B"), 0)))
        else:
            whole = gather_z(jnp.concatenate([shard, moved], axis=1))
            ff_w.append(((whole, 0), (whole, 1)))

    start = to_rel(tokens.reshape(rows, width), outer, b, c)
    ctx = jnp.pad(to_rel(context, outer, b, c), ((0, 0), (0, keys - cond), (0, 0)))
    ctx = ctx.reshape(slots * keys, -1)
    tables = rotary_tables(length)

    (n1,) = add_norm(start, None, None, norms, 0)
    keep_one, part = self_forward(n1, attn_w, tables, slots, groups)
    n2, h1 = add_norm(start, part, swap(part, T), norms, 1)
    keep_two, pair_rows, part = cross_forward(n2, ctx, cross_w, slots, cond, groups, block, pair_block)
    part = hold(part, ff_w[0][0][0], ff_w[1][0][0])
    n3, h2 = add_norm(h1, part, swap(part, T), norms, 2)
    n3_all = spread(n3, ff_w[1][1][0])

    n3_all = hold(n3_all, *[w[0][0] for w in ff_w])
    g_ff, dn3, y = [], [], []
    for i, blocks in enumerate(FF_BLOCKS):
        *grads, dn_part, y_part = feed_forward(
            n3_all, grad_all, ff_w[i][0], ff_w[i][1], blocks, FF_JOINT[i]
        )
        dn3.append(dn_part)
        y.append(y_part)
        if FF_JOINT[i]:
            g_ff.append(scatter_z(grads[0]).reshape(block, blocks, 2, 6 * UB))
        else:
            g_ff.append((grads[0], lax.ppermute(grads[1], "B", FLIP)))
    dn3 = collect(dn3).astype(BF16)

    out_half = collect(y) + by_core(h2)[0]
    out_half = (out_half * pick(t, live_rows[:half], live_rows[half:])).astype(BF16)
    out_half = lax.optimization_barrier(out_half)
    dn3 = from_core(dn3, swap(dn3, T))

    def ff_sum(keep, got):
        return scatter_z((keep.astype(F32) + got.astype(F32)).astype(BF16))

    dh2, dc, sums_three = norm_back(dn3, jnp.zeros_like(dn3), h2, grad_top, norms, 2)
    dc = hold(dc, out_half)
    *g_cross, dn2, dctx = cross_backward(
        dc, n2, ctx, keep_two, pair_rows, cross_w, slots, cond, groups, block, pair_block, CROSS_SCATTER[0]
    )
    g_cross = Scatter(CROSS_SCATTER, g_cross).first_far().first_near()
    dh1, da, sums_two = norm_back(dn2, swap(dn2, T), h1, dh2, norms, 1)
    da = hold(da, g_ff[2][1])
    mixed = restore(from_core(out_half, swap(hold(out_half, da), T)), b, c, outer)
    *g_attn, dn1 = self_backward(
        da, n1, keep_one, attn_w, tables, slots, groups, [order[0] for order in ATTN_SCATTER]
    )
    g_done = []
    for g in g_ff[:2]:
        far = lax.ppermute(hold(g[:, :, 1], dc), "B", FLIP)
        g_done.append((g[:, :, 0].astype(F32) + far.astype(F32)).astype(BF16).reshape(block, -1))
    g_done.append(ff_sum(hold(g_ff[2][0], da), g_ff[2][1]))
    dn1 = hold(dn1, g_cross.far[1], g_done[0])
    g_attn = [Scatter(order, g) for order, g in zip(ATTN_SCATTER, (g_attn[:4], g_attn[4:]))]
    for g in g_attn:
        g.first_far()
    g_cross.second()
    for g in g_attn:
        g.first_near()
    dtok, _, sums_one = norm_back(dn1, swap(dn1, T), start, dh1, norms, 0)
    dtok = restore(dtok, b, c, outer)

    sums = (sums_one, sums_two, sums_three)
    g_norm = jnp.concatenate([s[i : i + 1] for i in (0, 1) for s in sums], axis=0)
    g_norm = g_norm[:, : 2 * q4] + lax.ppermute(g_norm[:, 2 * q4 :], "C", FLIP)
    g_norm = g_norm[:, :q4] + lax.ppermute(g_norm[:, q4:], "B", FLIP)
    g_norm = jnp.pad(g_norm.T.astype(BF16), ((0, 0), (0, 128 - g_norm.shape[0])))
    g_norm = g_norm.reshape(outer, block, 128)
    g_norm = jnp.pad(g_norm, ((0, 0), (0, pair_block), (0, 0))).reshape(-1, 128)
    dctx = dctx.astype(F32) + swap(dctx, T).astype(F32)
    dctx = from_rel(dctx.reshape(slots, keys, -1)[:, :cond], outer, b, c)

    for g in g_attn:
        g.second()

    g_cross.kept = hold(g_cross.kept, *g_done)
    g_cross.kept = jnp.concatenate([g_cross.kept, g_norm], axis=1)
    g_cross = g_cross.third()
    g_norm = g_cross[:block, 2 * local :]
    g_cross = g_cross[:, : 2 * local]
    g_ff = jnp.concatenate(g_done, axis=1).reshape(block, part_blocks, 2, 3 * UB)
    own, far = g_ff[:, :, 0], lax.ppermute(g_ff[:, :, 1], "C", FLIP)
    g_ff = jnp.stack([pick(c, own, far), pick(c, far, own)], axis=1).astype(F32)
    g_ff = g_ff.reshape(block, 2, part_blocks, 3, UB).transpose(0, 3, 1, 2, 4)
    g_ff = g_ff.reshape(block, 3, units)
    g_gate_up, g_down = g_ff[:, :2], g_ff[:, 2].T
    g_attn = hold(jnp.concatenate([g.kept for g in g_attn], axis=1), mixed, dtok, dctx)
    g_attn = TAIL.run(scatter_z, g_attn).astype(F32)

    g_attn = g_attn.reshape(block, 2, groups, 2, GW).transpose(0, 1, 3, 2, 4).reshape(block, 4, local)
    g_cross = g_cross.reshape(block + pair_block, groups, 2, GW)
    g_pair = g_cross[block:].transpose(0, 2, 1, 3)
    g_cross = g_cross[:block]

    return (
        mixed.reshape(tokens.shape),
        dtok.reshape(tokens.shape),
        dctx,
        g_attn[:, :3],
        g_attn[:, 3].T,
        g_cross[:, :, 0].reshape(block, local),
        g_pair.reshape(pair_block, 2, local),
        g_cross[:, :, 1].reshape(block, local).T,
        g_gate_up,
        g_down,
        g_norm[:, :3].T,
        g_norm[:, 3:6].T,
    )


def solution(mesh):
    dp, tensor = mesh.devices.shape
    inner = Mesh(mesh.devices.reshape(dp // 4, 2, 2, tensor), DP + (T,))
    rows_dp = P(DP, None, None)
    weights = (
        P(DP, None, T),
        P(T, DP),
        P(DP, T),
        P(DP, None, T),
        P(T, DP),
        P(DP, None, T),
        P(T, DP),
        P(None, DP),
        P(None, DP),
    )
    return jax.shard_map(
        on_device,
        mesh=inner,
        in_specs=(rows_dp, rows_dp, P(DP), rows_dp) + weights,
        out_specs=(rows_dp, rows_dp, rows_dp) + weights,
        check_vma=False,
    )
```

```python
import functools

import jax
import jax.numpy as jnp
import numpy as np
from jax import lax
from jax.experimental import pallas as pl
from jax.experimental.pallas import tpu as pltpu
from jax.sharding import Mesh
from jax.sharding import PartitionSpec as P

HD = 64
ROT = 32
GROUP = 4
GW = GROUP * HD
UB = 256
EPSILON = 1e-05
SCALE = HD ** (-0.5)
F32 = jnp.float32
BF16 = jnp.bfloat16
DP = ("A", "B", "C")
T = "T"
FLIP = [(0, 1), (1, 0)]
AXIS = {"x": "C", "y": "B"}
VMEM_LIMIT = 58 * 1024 * 1024


class Lane:
    def __init__(self):
        self.last = None

    def run(self, move, value):
        if self.last is not None:
            value, _ = lax.optimization_barrier((value, self.last))
        self.last = move(value)
        return self.last


LANES = {}
TAIL = Lane()


def swap(value, axis):
    move = functools.partial(lax.ppermute, axis_name=axis, perm=FLIP)
    return LANES[axis].run(move, value) if axis in LANES else move(value)


def dot(left, right, dims):
    return lax.dot_general(left, right, (dims, ((), ())), preferred_element_type=F32)


def nn(left, right):
    return dot(left, right, ((1,), (0,)))


def nt(left, right):
    return dot(left, right, ((1,), (1,)))


def tn(left, right):
    return dot(left, right, ((0,), (0,)))


def pick(flag, when_zero, when_one):
    return jnp.where(flag == 0, when_zero, when_one)


def to_rel(values, outer, b, c):
    lead = values.shape[:-1]
    n = len(lead)
    v = values.reshape(lead + (outer, 2, 2, -1))
    v = jnp.transpose(v, tuple(range(n)) + (n + 2, n + 1, n, n + 3)).reshape(values.shape)
    return flip_blocks(v, b, c)


def flip_blocks(v, b, c):
    w = v.shape[-1]
    v = pick(c, v, jnp.concatenate([v[..., w // 2 :], v[..., : w // 2]], axis=-1))
    q = w // 4
    turned = [v[..., q : 2 * q], v[..., :q], v[..., 3 * q :], v[..., 2 * q : 3 * q]]
    return pick(b, v, jnp.concatenate(turned, axis=-1))


def from_rel(values, outer, b, c):
    lead = values.shape[:-1]
    n = len(lead)
    v = flip_blocks(values, b, c).reshape(lead + (2, 2, outer, -1))
    v = jnp.transpose(v, tuple(range(n)) + (n + 2, n + 1, n, n + 3))
    return v.reshape(values.shape)


def flip_half(values):
    half = values.shape[-1] // 2
    return jnp.concatenate([values[..., half:], values[..., :half]], axis=-1)


def gather_z(shard):
    return lax.all_gather(shard, "A", axis=0, tiled=True)


def scatter_z(rows):
    return lax.psum_scatter(rows, "A", scatter_dimension=0, tiled=True)


def hold(value, *others):
    return lax.optimization_barrier((value,) + others)[0]


def gather(shard, split, ready=()):
    first = gather_z(shard)
    over_y, over_x = swap(first, "B"), swap(first, "C")
    fourth = []
    from_y, from_x = (hold(over_y, *ready), hold(over_x, *ready)) if ready else (over_y, over_x)
    if split > 0:
        fourth.append((swap(from_y[:, :split], "C"), 0, split))
    if split < shard.shape[1]:
        fourth.append((swap(from_x[:, split:], "B"), split, shard.shape[1]))
    n = shard.shape[1]
    return {
        (0, 0): [(first, 0, n)],
        (0, 1): [(over_y, 0, n)],
        (1, 0): [(over_x, 0, n)],
        (1, 1): fourth,
    }


def columns(pieces, lo, width):
    found = []
    for p in PIECES:
        for a, begin, end in pieces[p]:
            if begin <= lo and lo + width <= end:
                found.append((a, (lo - begin) // width))
    return found


PIECES = ((0, 0), (0, 1), (1, 0), (1, 1))


class Scatter:
    def __init__(self, order, grads):
        self.order, self.grads = order, grads

    def first_far(self):
        self.far = (self.grads[2], swap(self.grads[3], AXIS[self.order[0]]))
        return self

    def first_near(self):
        self.near = (self.grads[0], swap(self.grads[1], AXIS[self.order[0]]))
        return self

    def second(self):
        far = (self.far[0].astype(F32) + self.far[1].astype(F32)).astype(BF16)
        moved = swap(far, AXIS[self.order[1]])
        near = self.near[0].astype(F32) + self.near[1].astype(F32)
        self.kept = (near + moved.astype(F32)).astype(BF16)
        return self

    def third(self):
        return TAIL.run(scatter_z, self.kept).astype(F32)


def full(array):
    nd = array.ndim
    return pl.BlockSpec(array.shape, lambda *_: (0,) * nd)


def piece_specs(found, n):
    return [pl.BlockSpec((a.shape[0], n), functools.partial(lambda i, *_: (0, i), i)) for a, i in found]


def piece_args(found):
    return [a for a, _ in found]


def call(body, outs, ins, specs, out_specs, grid=(1,), scratch=(), flops=0, name=None):
    moved = sum(int(np.prod(o.shape)) * o.dtype.itemsize for o in outs)
    moved += sum(int(np.prod(i.shape)) * i.dtype.itemsize for i in ins)
    return pl.pallas_call(
        body,
        out_shape=outs,
        grid=grid,
        in_specs=specs,
        out_specs=out_specs,
        scratch_shapes=list(scratch),
        compiler_params=pltpu.CompilerParams(
            dimension_semantics=("arbitrary",) * len(grid), vmem_limit_bytes=VMEM_LIMIT
        ),
        cost_estimate=pl.CostEstimate(flops=1, transcendentals=0, bytes_accessed=1),
        name=name,
    )(*ins)


def shape(dims, dtype):
    return jax.ShapeDtypeStruct(dims, dtype)


def head_masks(value):
    lane = lax.broadcasted_iota(jnp.int32, (1, GW), 1) // HD
    return [jnp.where(lane == h, value, 0.0).astype(BF16) for h in range(GROUP)]


def probabilities(qm, k, bias):
    scores = nt(qm, k)
    if bias is not None:
        scores = scores + bias
    top = jnp.max(scores, axis=-1, keepdims=True)
    e = jnp.exp(scores - top)
    return e * (1.0 / jnp.sum(e, axis=-1, keepdims=True))


def attention(q, k, v, bias):
    out = None
    for m, s in zip(head_masks(1.0), head_masks(SCALE)):
        p = probabilities(q * s, k, bias).astype(BF16)
        o = nn(p, v * m)
        out = o if out is None else out + o
    return out


def attention_back(q, k, v, do, bias):
    dq = dk = dv = None
    for m, s in zip(head_masks(1.0), head_masks(SCALE)):
        qm = q * s
        p = probabilities(qm, k, bias)
        dom = do * m
        dp = nt(dom, v)
        centre = jnp.sum(p * dp, axis=-1, keepdims=True)
        ds = (p * (dp - centre)).astype(BF16)
        a, b, c = nn(ds, k * s), tn(ds, qm), tn(p.astype(BF16), dom)
        dq, dk, dv = (a, b, c) if dq is None else (dq + a, dk + b, dv + c)
    return (dq, dk, dv)


def turn(u, cos, sin_a, sin_b):
    return u * cos + pltpu.roll(u, GW - ROT // 2, 1) * sin_a + pltpu.roll(u, ROT // 2, 1) * sin_b


def rotary_tables(length):
    half_dim = ROT // 2
    freqs = 10000.0 ** (-(2.0 * jnp.arange(half_dim, dtype=F32) / ROT))
    angles = jnp.arange(length, dtype=F32)[:, None] * freqs[None, :]
    cos, sin = jnp.cos(angles), jnp.sin(angles)
    rest = jnp.zeros((length, HD - ROT), F32)
    none = jnp.zeros_like(sin)
    return tuple(
        jnp.tile(jnp.concatenate(parts, axis=1), (1, GROUP))
        for parts in ((cos, cos, rest + 1.0), (-sin, none, rest), (none, sin, rest))
    )


def norm_rows(pieces, at, outer_rows):
    found = columns(pieces, at, 128)

    def body(*refs):
        for i in range(4):
            refs[4][:, i * outer_rows : (i + 1) * outer_rows] = refs[i][...].astype(F32).T[:8, :]

    out = shape((8, 4 * outer_rows), F32)
    return call(body, [out], piece_args(found), piece_specs(found, 128), [full(out)], name="norm_rows")[0]


def restore(values, turned_b, turned_c, outer):
    rows, width = values.shape
    block = width // (4 * outer)
    h, q = width // 2, width // 4
    step = 128

    def body(b_ref, c_ref, v_ref, out_ref):
        v = v_ref[...]
        v = jnp.where(c_ref[0] == 0, v, jnp.concatenate([v[:, h:], v[:, :h]], axis=1))
        turned = [v[:, q : 2 * q], v[:, :q], v[:, 3 * q :], v[:, 2 * q : 3 * q]]
        v = jnp.where(b_ref[0] == 0, v, jnp.concatenate(turned, axis=1))
        out_ref[...] = jnp.concatenate(
            [
                v[:, (2 * c + b) * q + a * block : (2 * c + b) * q + (a + 1) * block]
                for a in range(outer)
                for b in range(2)
                for c in range(2)
            ],
            axis=1,
        )

    row = pl.BlockSpec((step, width), lambda i: (i, 0))
    flag = pl.BlockSpec(memory_space=pltpu.SMEM)
    return call(
        body,
        [shape((rows, width), values.dtype)],
        [turned_b.reshape(1), turned_c.reshape(1), values],
        [flag, flag, row],
        [row],
        grid=(rows // step,),
        name="restore",
    )[0]


def add_norm(base, mine, other, norms, index):
    rows, width = base.shape
    step = 256
    extra = [] if mine is None else [mine, other]

    def body(*refs):
        base_ref, norm_ref = refs[0], refs[1]
        h = base_ref[...].astype(F32)
        if extra:
            h = h + (refs[2][...].astype(F32) + refs[3][...].astype(F32))
        outs = refs[2 + len(extra) :]
        average = jnp.mean(h, axis=-1, keepdims=True)
        centred = h - average
        spread = jnp.mean(centred * centred, axis=-1, keepdims=True)
        normed = centred * lax.rsqrt(spread + EPSILON)
        gain = norm_ref[index : index + 1, :]
        shift = norm_ref[index + 3 : index + 4, :]
        outs[0][...] = (normed * gain + shift).astype(BF16)
        if extra:
            outs[1][...] = h

    row = pl.BlockSpec((step, width), lambda i: (i, 0))
    outs = [shape((rows, width), BF16)] + ([shape((rows, width), F32)] if extra else [])
    return call(
        body,
        outs,
        [base, norms] + extra,
        [row, full(norms)] + [row] * len(extra),
        [row] * len(outs),
        grid=(rows // step,),
        flops=rows * width * 12,
        name="add_norm",
    )


def norm_back(mine, other, h, above, norms, index):
    rows, width = h.shape
    step = 256

    def body(mine_ref, other_ref, h_ref, above_ref, norm_ref, out_ref, low_ref, sums_ref):
        dn = mine_ref[...].astype(F32) + other_ref[...].astype(F32)
        h = h_ref[...].astype(F32)
        average = jnp.mean(h, axis=-1, keepdims=True)
        centred = h - average
        spread = jnp.mean(centred * centred, axis=-1, keepdims=True)
        factor = lax.rsqrt(spread + EPSILON)
        normed = centred * factor
        scaled = dn * norm_ref[index : index + 1, :]
        first = jnp.mean(scaled, axis=-1, keepdims=True)
        second = jnp.mean(scaled * normed, axis=-1, keepdims=True)
        d = above_ref[...].astype(F32) + factor * (scaled - first - normed * second)
        out_ref[...] = d
        low_ref[...] = d.astype(BF16)

        @pl.when(pl.program_id(0) == 0)
        def _():
            sums_ref[...] = jnp.zeros_like(sums_ref)

        sums_ref[0:1, :] += jnp.sum(dn * normed, axis=0, keepdims=True)
        sums_ref[1:2, :] += jnp.sum(dn, axis=0, keepdims=True)

    row = pl.BlockSpec((step, width), lambda i: (i, 0))
    return call(
        body,
        [shape((rows, width), F32), shape((rows, width), BF16), shape((8, width), F32)],
        [mine, other, h, above, norms],
        [row, row, row, row, full(norms)],
        [row, row, pl.BlockSpec((8, width), lambda i: (0, 0))],
        grid=(rows // step,),
        flops=rows * width * 20,
        name="norm_back",
    )


def grouped_specs(pieces, n):
    out = []
    for p in PIECES:
        for a, begin, end in pieces[p]:
            lo, count = begin // n, (end - begin) // n
            pick_block = functools.partial(
                lambda lo, count, j: (0, jnp.clip(j - lo, 0, count - 1)), lo, count
            )
            out.append((a, pl.BlockSpec((a.shape[0], n), pick_block), lo, lo + count))
    return out


def load_grouped(found, refs, w, rows):
    j = pl.program_id(0)
    at = -rows
    for (_, _, lo, hi), r in zip(found, refs):
        if lo == 0:
            at += rows
        target = slice(at, at + rows)

        @pl.when((j >= lo) & (j < hi))
        def _(r=r, target=target):
            w[target, :] = r[...]


def constant(array):
    nd = array.ndim
    return pl.BlockSpec(array.shape, lambda *_: (0,) * nd, pipeline_mode=pl.Buffered(1))


def self_forward(n, pieces, tables, slots, groups):
    rows, width = n.shape
    length = rows // slots
    q4 = width // 4
    cols = 4 * GW
    found = grouped_specs(pieces, cols)

    def body(*refs):
        n_ref, w_refs, tabs = refs[0], refs[1 : 1 + len(found)], refs[1 + len(found) : 4 + len(found)]
        keep_ref, part_ref, w, raw, total = refs[4 + len(found) :]
        j = pl.program_id(0)
        load_grouped(found, w_refs, w, q4)
        raw[...] = nn(n_ref[...], w[:, : 3 * GW])
        cos, sin_a, sin_b = (r[...] for r in tabs)
        for l in range(slots):
            at = slice(l * length, (l + 1) * length)
            q = turn(raw[at, :GW], cos, sin_a, sin_b).astype(BF16)
            key = turn(raw[at, GW : 2 * GW], cos, sin_a, sin_b).astype(BF16)
            v = raw[at, 2 * GW :].astype(BF16)
            keep_ref[at, :GW] = q
            keep_ref[at, GW : 2 * GW] = key
            keep_ref[at, 2 * GW : 3 * GW] = v
            keep_ref[at, 3 * GW :] = attention(q, key, v, None).astype(BF16)
        part = nt(keep_ref[:, 3 * GW :], w[:, 3 * GW :])

        @pl.when(j == 0)
        def _():
            total[...] = part

        @pl.when(j > 0)
        def _():
            total[...] += part

        @pl.when(j == pl.num_programs(0) - 1)
        def _():
            part_ref[...] = total[...].astype(BF16)

    ins = [n] + [f[0] for f in found] + list(tables)
    specs = [constant(n)] + [f[1] for f in found] + [constant(a) for a in tables]
    outs = [shape((rows, groups * cols), BF16), shape((rows, width), BF16)]
    return call(
        body,
        outs,
        ins,
        specs,
        [pl.BlockSpec((rows, cols), lambda j: (0, j)), full(outs[1])],
        grid=(groups,),
        scratch=[
            pltpu.VMEM((width, cols), BF16),
            pltpu.VMEM((rows, 3 * GW), F32),
            pltpu.VMEM((rows, width), F32),
        ],
        name="self_forward",
    )


def load_cross(w_refs, w, wp, at, block, pair_block):
    both = block + pair_block
    outer = w_refs[0][0].shape[0] // both
    for i, parts in enumerate(w_refs):
        for o in range(outer):
            r = parts[0]
            w[(i * outer + o) * block : (i * outer + o + 1) * block, at] = r[o * both : o * both + block, :]
            wp[(i * outer + o) * pair_block : (i * outer + o + 1) * pair_block, at] = r[
                o * both + block : (o + 1) * both, :
            ]


def cross_operands(pieces, groups):
    found = [columns(pieces, j * 2 * GW, 2 * GW) for j in range(groups)]
    return [a for f in found for a in piece_args(f)], [q for f in found for q in piece_specs(f, 2 * GW)]


def cross_forward(n, ctx, pieces, slots, cond, groups, block, pair_block):
    rows, width = n.shape
    length, keys = rows // slots, ctx.shape[0] // slots
    cols = groups * 2 * GW

    def body(n_ref, ctx_ref, *refs):
        w_refs = refs[: 4 * groups]
        keep_ref, pair_ref, part_ref, w, wp, cq = refs[4 * groups :]
        lane = lax.broadcasted_iota(jnp.int32, (1, keys), 1)
        bias = jnp.where(lane < cond, 0.0, -1e30).astype(F32)
        part = None
        for j in range(groups):
            at_j = slice(2 * j * GW, 2 * (j + 1) * GW)
            load_cross([[r] for r in w_refs[4 * j : 4 * j + 4]], w, wp, at_j, block, pair_block)
            at_q = slice(2 * j * GW, (2 * j + 1) * GW)
            at_o = slice((2 * j + 1) * GW, (2 * j + 2) * GW)
            pair_ref[:, at_j] = nn(ctx_ref[...], wp[:, at_j]).astype(BF16)
            cq[...] = nn(n_ref[...], w[:, at_q]).astype(BF16)
            keep_ref[:, at_q] = cq[...]
            for l in range(slots):
                at = slice(l * length, (l + 1) * length)
                at_k = slice(l * keys, (l + 1) * keys)
                o = attention(cq[at, :], pair_ref[at_k, at_q], pair_ref[at_k, at_o], bias)
                keep_ref[at, at_o] = o.astype(BF16)
            more = nt(keep_ref[:, at_o], w[:, at_o])
            part = more if part is None else part + more
        part_ref[...] = part.astype(BF16)

    more_ins, more_specs = cross_operands(pieces, groups)
    ins = [n, ctx] + more_ins
    specs = [full(n), full(ctx)] + more_specs
    outs = [
        shape((rows, cols), BF16),
        shape((slots * keys, cols), BF16),
        shape((rows, width), BF16),
    ]
    return call(
        body,
        outs,
        ins,
        specs,
        [full(o) for o in outs],
        scratch=[
            pltpu.VMEM((width, cols), BF16),
            pltpu.VMEM((ctx.shape[1], cols), BF16),
            pltpu.VMEM((rows, GW), BF16),
        ],
        flops=2 * rows * width * cols + 2 * ctx.shape[0] * ctx.shape[1] * cols,
        name="cross_forward",
    )


def feed_forward(x, d, near_w, far_w, blocks, joint):
    rows, width = x.shape
    q4 = width // 4
    cols = 6 * UB

    def body(*refs):
        if not joint:
            x_ref, d_ref, a_ref, b_ref, keep_ref, send_ref, dn_ref, y_ref, w, dn, y = refs
        else:
            x_ref, d_ref, a_ref, b_ref, keep_ref, dn_ref, y_ref, w, dn, y = refs
        j = pl.program_id(0)
        for rx in range(2):
            for ry, r in enumerate((a_ref, b_ref)):
                at = (2 * rx + ry) * q4
                w[at : at + q4, :] = r[:, rx * 3 * UB : (rx + 1) * 3 * UB]
        gu = nn(x_ref[...], w[:, : 2 * UB])
        dh = nn(d_ref[...], w[:, 2 * UB :])
        gate, upper = gu[:, :UB], gu[:, UB:]
        sig = 1.0 / (1.0 + jnp.exp(-gate))
        silu = gate * sig
        hidden = (silu * upper).astype(BF16)
        dg = (dh * upper * (sig * (1.0 + gate * (1.0 - sig)))).astype(BF16)
        du = (dh * silu).astype(BF16)
        dgu = jnp.concatenate([dg, du], axis=1)
        for rx in range(2):
            for ref, right, lo, n in ((x_ref, dgu, 0, 2 * UB), (d_ref, hidden, 2 * UB, UB)):
                c0 = 2 * rx * q4
                at = slice(rx * 3 * UB + lo, rx * 3 * UB + lo + n)
                near = tn(ref[:, c0 : c0 + q4], right)
                far = tn(ref[:, c0 + q4 : c0 + 2 * q4], right)
                keep_ref[:, at] = near.astype(BF16)
                if joint:
                    keep_ref[:, cols + at.start : cols + at.stop] = far.astype(BF16)
                else:
                    send_ref[:, at] = far.astype(BF16)
        more_dn = nt(dgu, w[:, : 2 * UB])
        more_y = nt(hidden, w[:, 2 * UB :])

        @pl.when(j == 0)
        def _():
            dn[...] = more_dn
            y[...] = more_y

        @pl.when(j > 0)
        def _():
            dn[...] += more_dn
            y[...] += more_y

        @pl.when(j == pl.num_programs(0) - 1)
        def _():
            dn_ref[...] = dn[...].astype(BF16)
            y_ref[...] = y[...].astype(BF16)

    block = pl.BlockSpec((q4, cols), lambda j: (0, j))
    from_w = [
        pl.BlockSpec((q4, cols), functools.partial(lambda i, j: (0, i + j), i * blocks))
        for _, i in (near_w, far_w)
    ]
    ins = [x, d, near_w[0], far_w[0]]
    specs = [constant(x), constant(d)] + from_w
    if joint:
        outs = [shape((q4, 2 * blocks * cols), BF16)]
        out_specs = [pl.BlockSpec((q4, 2 * cols), lambda j: (0, j))]
    else:
        outs = [shape((q4, blocks * cols), BF16)] * 2
        out_specs = [block, block]
    sums = [shape((rows, width), BF16)] * 2
    return call(
        body,
        outs + sums,
        ins,
        specs,
        out_specs + [full(o) for o in sums],
        grid=(blocks,),
        scratch=[
            pltpu.VMEM((width, 3 * UB), BF16),
            pltpu.VMEM((rows, width), F32),
            pltpu.VMEM((rows, width), F32),
        ],
        flops=18 * rows * width * UB * blocks,
        name="feed_forward",
    )


def split_rows(left_ref, right, first, grads, cols, outer=1, at_row=0):
    q = left_ref.shape[1] // 4
    run = grads[0].shape[0] // outer
    part = q // outer
    for rx, ry in PIECES:
        g = tn(left_ref[:, (2 * rx + ry) * q : (2 * rx + ry + 1) * q], right).astype(BF16)
        goes, other = (rx, ry) if first == "x" else (ry, rx)
        for o in range(outer):
            grads[2 * other + goes][o * run + at_row : o * run + at_row + part, cols] = g[
                o * part : (o + 1) * part, :
            ]


def cross_backward(dc, n, ctx, keep, pair_rows, pieces, slots, cond, groups, block, pair_block, first):
    rows, width = n.shape
    length, keys = rows // slots, ctx.shape[0] // slots
    cols = keep.shape[1]
    outer = width // 4 // block

    def body(dc_ref, n_ref, ctx_ref, keep_in, pair_in, *refs):
        w_refs = refs[: 4 * groups]
        grads, (dn_ref, dctx_ref, w, wp, do, dcq, dpair) = refs[4 * groups : 4 * groups + 4], refs[4 * groups + 4 :]
        lane = lax.broadcasted_iota(jnp.int32, (1, keys), 1)
        bias = jnp.where(lane < cond, 0.0, -1e30).astype(F32)
        dn = None
        for j in range(groups):
            at_j = slice(2 * j * GW, 2 * (j + 1) * GW)
            load_cross([[r] for r in w_refs[4 * j : 4 * j + 4]], w, wp, at_j, block, pair_block)
            at_q = slice(2 * j * GW, (2 * j + 1) * GW)
            at_o = slice((2 * j + 1) * GW, (2 * j + 2) * GW)
            do[...] = nn(dc_ref[...], w[:, at_o]).astype(BF16)
            for l in range(slots):
                at = slice(l * length, (l + 1) * length)
                at_k = slice(l * keys, (l + 1) * keys)
                a, b, c = attention_back(
                    keep_in[at, at_q], pair_in[at_k, at_q], pair_in[at_k, at_o], do[at, :], bias
                )
                dcq[at, :] = a.astype(BF16)
                dpair[at_k, at_q] = b.astype(BF16)
                dpair[at_k, at_o] = c.astype(BF16)
            more = nt(dcq[...], w[:, at_q])
            dn = more if dn is None else dn + more
            split_rows(n_ref, dcq[...], first, grads, at_q, outer)
            split_rows(dc_ref, keep_in[:, at_o], first, grads, at_o, outer)
            split_rows(ctx_ref, dpair[:, at_j], first, grads, at_j, outer, block)
        dn_ref[...] = dn.astype(BF16)
        dctx_ref[...] = nt(dpair[...], wp[...]).astype(BF16)

    more_ins, more_specs = cross_operands(pieces, groups)
    ins = [dc, n, ctx, keep, pair_rows] + more_ins
    specs = [full(a) for a in ins[:5]] + more_specs
    grad_rows = outer * (block + pair_block)
    outs = [shape((grad_rows, cols), BF16)] * 4 + [shape((rows, width), BF16), shape(ctx.shape, BF16)]
    return call(
        body,
        outs,
        ins,
        specs,
        [full(o) for o in outs],
        scratch=[
            pltpu.VMEM((width, cols), BF16),
            pltpu.VMEM((ctx.shape[1], cols), BF16),
            pltpu.VMEM((rows, GW), BF16),
            pltpu.VMEM((rows, GW), BF16),
            pltpu.VMEM((slots * keys, cols), BF16),
        ],
        flops=4 * rows * width * cols + 4 * ctx.shape[0] * ctx.shape[1] * cols,
        name="cross_backward",
    )


def self_backward(da, n, keep, pieces, tables, slots, groups, firsts):
    rows, width = n.shape
    length = rows // slots
    q4 = width // 4
    cols = 4 * GW
    found = grouped_specs(pieces, cols)

    def body(*refs):
        da_ref, n_ref, keep_in = refs[:3]
        w_refs, tabs = refs[3 : 3 + len(found)], refs[3 + len(found) : 6 + len(found)]
        grads = [refs[6 + len(found) : 10 + len(found)], refs[10 + len(found) : 14 + len(found)]]
        dn_ref, w, do, dt, total = refs[14 + len(found) :]
        j = pl.program_id(0)
        load_grouped(found, w_refs, w, q4)
        do[...] = nn(da_ref[...], w[:, 3 * GW :]).astype(BF16)
        cos, sin_a, sin_b = (r[...] for r in tabs)
        for l in range(slots):
            at = slice(l * length, (l + 1) * length)
            dq, dk, dv = attention_back(
                keep_in[at, :GW], keep_in[at, GW : 2 * GW], keep_in[at, 2 * GW : 3 * GW], do[at, :], None
            )
            dt[at, :GW] = turn(dq, cos, -sin_a, -sin_b).astype(BF16)
            dt[at, GW : 2 * GW] = turn(dk, cos, -sin_a, -sin_b).astype(BF16)
            dt[at, 2 * GW :] = dv.astype(BF16)
        split_rows(n_ref, dt[:, : 2 * GW], firsts[0], grads[0], slice(0, 2 * GW))
        split_rows(n_ref, dt[:, 2 * GW :], firsts[1], grads[1], slice(0, GW))
        split_rows(da_ref, keep_in[:, 3 * GW :], firsts[1], grads[1], slice(GW, 2 * GW))
        dn = nt(dt[...], w[:, : 3 * GW])

        @pl.when(j == 0)
        def _():
            total[...] = dn

        @pl.when(j > 0)
        def _():
            total[...] += dn

        @pl.when(j == pl.num_programs(0) - 1)
        def _():
            dn_ref[...] = total[...].astype(BF16)

    ins = [da, n, keep] + [f[0] for f in found] + list(tables)
    step = pl.BlockSpec((rows, cols), lambda j: (0, j))
    specs = [constant(da), constant(n), step] + [f[1] for f in found] + [constant(a) for a in tables]
    outs = [shape((q4, groups * cols // 2), BF16)] * 8 + [shape((rows, width), BF16)]
    grad = pl.BlockSpec((q4, cols // 2), lambda j: (0, j))
    return call(
        body,
        outs,
        ins,
        specs,
        [grad] * 8 + [full(outs[8])],
        grid=(groups,),
        scratch=[
            pltpu.VMEM((width, cols), BF16),
            pltpu.VMEM((rows, GW), BF16),
            pltpu.VMEM((rows, 3 * GW), BF16),
            pltpu.VMEM((rows, width), F32),
        ],
        name="self_backward",
    )


ATTN_SPLIT = 2
CROSS_SPLIT = 1
FF_BLOCKS = (2, 2, 2)
FF_EARLY_Y = (True, False, False)
FF_JOINT = (True, True, False)
ATTN_SCATTER = ("yxz", "xyz")
CROSS_SCATTER = "xyz"


def on_device(
    tokens,
    context,
    live_count,
    cotangent,
    triple_weight,
    attn_out_weight,
    cross_query_weight,
    cross_pair_weight,
    cross_out_weight,
    gate_up_weight,
    down_weight,
    norm_gains,
    norm_shifts,
):
    LANES.clear()
    TAIL.last = None
    LANES.update({name: Lane() for name in DP[1:]})
    b = lax.axis_index("B")
    c = lax.axis_index("C")
    t = lax.axis_index(T)
    outer = lax.axis_size("A")
    slots, length, width = tokens.shape
    rows = slots * length
    half = rows // 2
    cond = context.shape[1]
    keys = -(-cond // 16) * 16
    block = triple_weight.shape[0]
    pair_block = cross_pair_weight.shape[0]
    local = triple_weight.shape[2]
    groups = local // GW
    units = gate_up_weight.shape[2]
    part_blocks = units // 2 // UB
    q4 = width // 4

    def group(w, j):
        return w[..., j * GW : (j + 1) * GW]

    live = (live_count[0] > jnp.arange(slots)).astype(F32)
    live_rows = jnp.repeat(live, length)[:, None]

    def by_core(value):
        return (
            pick(t, value[:half], value[half:]),
            pick(t, value[half:], value[:half]),
        )

    def from_core(mine, other):
        return jnp.concatenate([pick(t, mine, other), pick(t, other, mine)], axis=0)

    def spread(value, *others):
        mine, other = by_core(value)
        far = flip_half(swap(mine, "C"))
        if others:
            far = hold(far, *others)
        return jnp.concatenate([mine, far, other, swap(far, T)], axis=0)

    def collect(parts):
        total = sum(p.astype(F32) for p in parts)
        got = total[:rows] + swap(total[rows:].astype(BF16), T).astype(F32)
        return got[:half] + swap(flip_half(got[half:].astype(BF16)), "C").astype(F32)

    attn_t, cross_t = attn_out_weight.T, cross_out_weight.T
    norm_in = jnp.concatenate([norm_gains, norm_shifts], axis=0).T
    attn_in = jnp.concatenate(
        [group(w, j) for j in range(groups) for w in [triple_weight[:, k] for k in range(3)] + [attn_t]]
        + [jnp.pad(norm_in, ((0, 0), (0, 128 - norm_in.shape[1])))],
        axis=1,
    )
    cross_in = jnp.concatenate(
        [
            jnp.concatenate(
                [group(w, j) for j in range(groups) for w in (cross_query_weight, cross_t)], axis=1
            ),
            jnp.concatenate(
                [group(cross_pair_weight[:, k], j) for j in range(groups) for k in range(2)], axis=1
            ),
        ],
        axis=0,
    )
    ff = jnp.concatenate([gate_up_weight, down_weight.T[:, None]], axis=1)
    ff = ff.reshape(block, 3, 2, part_blocks, UB).transpose(2, 0, 3, 1, 4)
    ff = ff.reshape(2, block, part_blocks, 3 * UB)
    ff_own = pick(c, ff[0], ff[1])
    ff_far = swap(pick(c, ff[1], ff[0]), "C")
    ff_in = jnp.stack([ff_own, ff_far], axis=2).reshape(block, part_blocks * 6 * UB)

    early = []
    at = 0
    for blocks, soon in zip(FF_BLOCKS, FF_EARLY_Y):
        shard = ff_in[:, at : at + blocks * 6 * UB]
        at += blocks * 6 * UB
        early.append((shard, swap(shard, "B") if soon else None))
    grad_top = to_rel(cotangent.reshape(rows, width), outer, b, c) * live_rows.astype(BF16)
    start = to_rel(tokens.reshape(rows, width), outer, b, c)
    ctx = jnp.pad(to_rel(context, outer, b, c), ((0, 0), (0, keys - cond), (0, 0)))
    ctx = ctx.reshape(slots * keys, -1)
    tables = rotary_tables(length)
    attn_w = gather(attn_in, ATTN_SPLIT * 4 * GW, (start, ctx) + tables)
    cross_w = gather(cross_in, CROSS_SPLIT * 2 * GW, (grad_top,))
    grad_all = spread(grad_top)
    norm_at = groups * 4 * GW
    norms = norm_rows(attn_w, norm_at, q4)
    ff_w = []
    for shard, moved in early:
        if moved is None:
            near = gather_z(shard)
            ff_w.append(((near, 0), (swap(near, "B"), 0)))
        else:
            whole = gather_z(jnp.concatenate([shard, moved], axis=1))
            ff_w.append(((whole, 0), (whole, 1)))


    (n1,) = add_norm(start, None, None, norms, 0)
    keep_one, part = self_forward(n1, attn_w, tables, slots, groups)
    n2, h1 = add_norm(start, part, swap(part, T), norms, 1)
    keep_two, pair_rows, part = cross_forward(n2, ctx, cross_w, slots, cond, groups, block, pair_block)
    part = hold(part, ff_w[0][0][0], ff_w[1][0][0])
    n3, h2 = add_norm(h1, part, swap(part, T), norms, 2)
    n3_all = spread(n3, ff_w[1][1][0])

    n3_all = hold(n3_all, *[w[0][0] for w in ff_w])
    g_ff, dn3, y = [], [], []
    for i, blocks in enumerate(FF_BLOCKS):
        *grads, dn_part, y_part = feed_forward(
            n3_all, grad_all, ff_w[i][0], ff_w[i][1], blocks, FF_JOINT[i]
        )
        dn3.append(dn_part)
        y.append(y_part)
        if FF_JOINT[i]:
            g_ff.append(scatter_z(grads[0]).reshape(block, blocks, 2, 6 * UB))
        else:
            g_ff.append((grads[0], lax.ppermute(grads[1], "B", FLIP)))
    dn3 = collect(dn3).astype(BF16)

    out_half = collect(y) + by_core(h2)[0]
    out_half = (out_half * pick(t, live_rows[:half], live_rows[half:])).astype(BF16)
    out_half = lax.optimization_barrier(out_half)
    dn3 = from_core(dn3, swap(dn3, T))

    def ff_sum(keep, got):
        return scatter_z((keep.astype(F32) + got.astype(F32)).astype(BF16))

    dh2, dc, sums_three = norm_back(dn3, jnp.zeros_like(dn3), h2, grad_top, norms, 2)
    dc = hold(dc, out_half)
    *g_cross, dn2, dctx = cross_backward(
        dc, n2, ctx, keep_two, pair_rows, cross_w, slots, cond, groups, block, pair_block, CROSS_SCATTER[0]
    )
    g_cross = Scatter(CROSS_SCATTER, g_cross).first_far().first_near()
    dh1, da, sums_two = norm_back(dn2, swap(dn2, T), h1, dh2, norms, 1)
    da = hold(da, g_ff[2][1])
    mixed = restore(from_core(out_half, swap(hold(out_half, da), T)), b, c, outer)
    *g_attn, dn1 = self_backward(
        da, n1, keep_one, attn_w, tables, slots, groups, [order[0] for order in ATTN_SCATTER]
    )
    g_done = []
    for g in g_ff[:2]:
        far = lax.ppermute(hold(g[:, :, 1], dc), "B", FLIP)
        g_done.append((g[:, :, 0].astype(F32) + far.astype(F32)).astype(BF16).reshape(block, -1))
    g_done.append(ff_sum(hold(g_ff[2][0], da), g_ff[2][1]))
    dn1 = hold(dn1, g_cross.far[1], g_done[0])
    g_attn = [Scatter(order, g) for order, g in zip(ATTN_SCATTER, (g_attn[:4], g_attn[4:]))]
    for g in g_attn:
        g.first_far()
    g_cross.second()
    for g in g_attn:
        g.first_near()
    dtok, _, sums_one = norm_back(dn1, swap(dn1, T), start, dh1, norms, 0)
    dtok = restore(dtok, b, c, outer)

    sums = (sums_one, sums_two, sums_three)
    g_norm = jnp.concatenate([s[i : i + 1] for i in (0, 1) for s in sums], axis=0)
    g_norm = g_norm[:, : 2 * q4] + lax.ppermute(g_norm[:, 2 * q4 :], "C", FLIP)
    g_norm = g_norm[:, :q4] + lax.ppermute(g_norm[:, q4:], "B", FLIP)
    g_norm = jnp.pad(g_norm.T.astype(BF16), ((0, 0), (0, 128 - g_norm.shape[0])))
    g_norm = g_norm.reshape(outer, block, 128)
    g_norm = jnp.pad(g_norm, ((0, 0), (0, pair_block), (0, 0))).reshape(-1, 128)
    dctx = dctx.astype(F32) + swap(dctx, T).astype(F32)
    dctx = from_rel(dctx.reshape(slots, keys, -1)[:, :cond], outer, b, c)

    for g in g_attn:
        g.second()

    g_cross.kept = hold(g_cross.kept, *g_done)
    g_cross.kept = jnp.concatenate([g_cross.kept, g_norm], axis=1)
    g_cross = g_cross.third()
    g_norm = g_cross[:block, 2 * local :]
    g_cross = g_cross[:, : 2 * local]
    g_ff = jnp.concatenate(g_done, axis=1).reshape(block, part_blocks, 2, 3 * UB)
    own, far = g_ff[:, :, 0], lax.ppermute(g_ff[:, :, 1], "C", FLIP)
    g_ff = jnp.stack([pick(c, own, far), pick(c, far, own)], axis=1).astype(F32)
    g_ff = g_ff.reshape(block, 2, part_blocks, 3, UB).transpose(0, 3, 1, 2, 4)
    g_ff = g_ff.reshape(block, 3, units)
    g_gate_up, g_down = g_ff[:, :2], g_ff[:, 2].T
    g_attn = hold(jnp.concatenate([g.kept for g in g_attn], axis=1), mixed, dtok, dctx)
    g_attn = TAIL.run(scatter_z, g_attn).astype(F32)

    g_attn = g_attn.reshape(block, 2, groups, 2, GW).transpose(0, 1, 3, 2, 4).reshape(block, 4, local)
    g_cross = g_cross.reshape(block + pair_block, groups, 2, GW)
    g_pair = g_cross[block:].transpose(0, 2, 1, 3)
    g_cross = g_cross[:block]

    return (
        mixed.reshape(tokens.shape),
        dtok.reshape(tokens.shape),
        dctx,
        g_attn[:, :3],
        g_attn[:, 3].T,
        g_cross[:, :, 0].reshape(block, local),
        g_pair.reshape(pair_block, 2, local),
        g_cross[:, :, 1].reshape(block, local).T,
        g_gate_up,
        g_down,
        g_norm[:, :3].T,
        g_norm[:, 3:6].T,
    )


def solution(mesh):
    dp, tensor = mesh.devices.shape
    inner = Mesh(mesh.devices.reshape(dp // 4, 2, 2, tensor), DP + (T,))
    rows_dp = P(DP, None, None)
    weights = (
        P(DP, None, T),
        P(T, DP),
        P(DP, T),
        P(DP, None, T),
        P(T, DP),
        P(DP, None, T),
        P(T, DP),
        P(None, DP),
        P(None, DP),
    )
    return jax.shard_map(
        on_device,
        mesh=inner,
        in_specs=(rows_dp, rows_dp, P(DP), rows_dp) + weights,
        out_specs=(rows_dp, rows_dp, rows_dp) + weights,
        check_vma=False,
    )
```
